256 devices in a mesh: cell: 16 (over z, core), sub: 16 (over x, y).
Axes of the slice: x: 4, y: 4, z: 8, core: 2. Of those that a mesh axis runs over, the one named last changes fastest.
Arguments:
- queries: bfloat16 [4096, 1024], P('cell', 'sub'), may hold values from -384 to 384
- probe_groups: int32 [4096, 2], P('cell'), may hold values from 0 to 15, all different within a row; in each aligned block of 256 rows (0 to 255, 256 to 511, ...) at most 64 rows name the same one
- probe_cells: int32 [4096, 2, 16], P('cell'), may hold values from 0 to 31, as said below
- coarse: bfloat16 [512, 1024], P('cell', 'sub'), may hold values from -1.1953125 to 1.1953125
- codebooks: bfloat16 [64, 16, 256], P('sub'), may hold values from -1.5 to 1.5
- codes: int32 [512, 64, 384], P('cell', 'sub'), may hold values from 0 to 255
- lengths: int32 [512], P('cell'), may hold values from 1 to 384, 98304 in all
- payload: bfloat16 [512, 384, 256], P('cell', 'sub'), may hold values from -6 to 6
Outputs:
- pooled: bfloat16 [4096, 256], P('cell')
The draws below stay inside these ranges and needn't reach their ends.
Inputs may be any that keep to these rules, and one draw needn't show every extreme that they name: `probe_cells`: the 16 cells of one query in one group are distinct. `probe_groups`: the queries of one index of cell name one group at most 64 times, and one group exactly 64 times in some index. `lengths`: some cell has all 384 rows live.
All inputs are finite; a program needn't handle non-finite values. No bound on the sum of `lengths` on one device may be relied on, other than what follows from the above.
Results may differ from the reference program's by a relative error of at most 0.003.
The reference program's roundings to bfloat16 on the way count: a program that leaves them out, or rounds other values in their place, can miss the bound.
Values may be sent and summed in bfloat16 or wider, within the bound.
No kernel may reach another device: no remote copies, remote signals or barrier semaphores. Data moves between devices by JAX's collectives and lax.ppermute only.
A program may use at most 64 MiB of HBM per device.

```python
import math
import jax
import jax.numpy as jnp
import numpy as np
from jax import lax

M = 64
SD = 16
K = 256
PW = 256
HALF = 16
CELL_DEV = 32
ROWS = 384
Q_DEV = 256
CAP = 64
DIM = 1024
QUERIES = 4096
CELLS = 512
N_CELL = 16


def draw_queries(key, part):
    base = jnp.clip(jax.random.normal(key, (QUERIES, DIM), jnp.float32), -6.0, 6.0)
    return base.astype(jnp.bfloat16)


def draw_probe_cells(key, part):
    keys = jax.random.split(key, QUERIES * 2)
    picks = jax.vmap(lambda single: jax.random.permutation(single, CELL_DEV)[:HALF])(keys)
    return picks.reshape(QUERIES, 2, HALF).astype(jnp.int32)


def place_ends(array, key, least, top_value):
    spot = [jax.random.randint(jax.random.fold_in(key, axis), (), 0, length) for axis, length in enumerate(array.shape)]
    widest = array.shape.index(max(array.shape))
    beside = spot[:widest] + [(spot[widest] + 1) % array.shape[widest]] + spot[widest + 1:]
    return array.at[tuple(spot)].set(least).at[tuple(beside)].set(top_value)


def shard_levels(own_key, dims, cuts, low, top_value):
    def one(axis_at, blocks):
        steps = jax.random.uniform(jax.random.fold_in(jax.random.fold_in(own_key, 6), axis_at), (blocks,), jnp.float32, low / len(cuts), top_value / len(cuts))
        return jnp.repeat(jnp.exp(steps), dims[axis_at] // blocks).reshape((-1,) + (1,) * (len(dims) - axis_at - 1))

    gain = one(*cuts[0])
    for cut in cuts[1:]:
        gain = gain * one(*cut)
    return gain


def profile(amount, total, bound, slope):
    portions = [(1 << 20) // math.isqrt(rank ** slope) + 1 for rank in range(2, amount + 1)]
    spare, given = total - bound - (amount - 1), [1] * (amount - 1)
    while spare > 0:
        free = [i for i in range(amount - 1) if given[i] < bound]
        whole, left = sum([portions[i] for i in free]), spare
        for i in free:
            addition = min(bound - given[i], max(1, left * portions[i] // whole), spare)
            given[i] = given[i] + addition
            spare = spare - addition
    return np.array([bound] + given)


def uneven_parts(stream_key, number_of, total, most, skew):
    if number_of == 2:
        one = jax.random.randint(stream_key, (), max(1, total - most), min(most, total - 1) + 1)
        return jnp.stack([one, total - one])
    sizes = jnp.asarray(profile(number_of, total, most, skew), jnp.int32)
    couples = (number_of - 1) // 2
    source_of, sink = sizes[1:1 + 2 * couples:2], sizes[2:2 + 2 * couples:2]
    slack = jnp.minimum(source_of - 1, most - sink)
    passed = jax.random.randint(jax.random.fold_in(stream_key, 1), (couples,), 0, 1 << 20) % (slack + 1)
    sizes = sizes.at[1:1 + 2 * couples:2].set(source_of - passed).at[2:2 + 2 * couples:2].set(sink + passed)
    return sizes[jax.random.permutation(jax.random.fold_in(stream_key, 2), number_of)]


def routed_block(own_key, own, number, rows, amount, top, most, skew):
    ranking = jax.random.permutation(own_key, amount)
    crowded, ordinary = portions_of(amount, rows * top, most, skew, True), portions_of(amount, rows * top, most, skew, False)
    places = jnp.arange(amount)

    def named(sizes, offset_by):
        used = int((sizes > 0).sum())
        fixed = max(1, used // 4)
        shifted = fixed + (places - fixed + offset_by * (used - fixed)) % max(1, amount - fixed)
        return jnp.zeros((amount,), jnp.int32).at[ranking[jnp.where(places < fixed, places, shifted)]].set(jnp.asarray(sizes, jnp.int32))

    sizes = jnp.where(number % 4 == 0, named(crowded, number // 4), named(ordinary, number - number // 4 - 1))
    mixed = jax.random.permutation(jax.random.fold_in(own, 3), amount)
    donor, taker = mixed[0:amount // 2 * 2:2], mixed[1:amount // 2 * 2:2]
    room = jnp.minimum(sizes[donor] - 1, most - sizes[taker]) // 2
    room = jnp.where((donor == ranking[0]) | (taker == ranking[0]) | (sizes[taker] == 0), 0, jnp.maximum(room, 0))
    shifted = jax.random.randint(jax.random.fold_in(own, 4), (amount // 2,), 0, 1 << 20) % (room + 1)
    sizes = sizes.at[donor].add(-shifted).at[taker].add(shifted)
    items = jnp.searchsorted(jnp.cumsum(sizes), jnp.arange(rows * top), side="right").astype(jnp.int32)
    grid = items.reshape(top, rows).T
    grid = grid[jax.random.permutation(jax.random.fold_in(own, 1), rows)]
    offset_by = jax.random.randint(jax.random.fold_in(own, 2), (rows, 1), 0, top)
    return jnp.take_along_axis(grid, (jnp.arange(top)[None, :] + offset_by) % top, axis=1)


def portions_of(number_of, total, most, lean, full):
    portions = [(1 << 20) // math.isqrt(standing ** lean) + 1 for standing in range(1, number_of + 1)]
    largest = most if full else min(most, max(-(-total // number_of), total * portions[0] // sum(portions)))
    least = 1 if total - largest >= number_of - 1 else 0
    holding, surplus = [largest] + [least] * (number_of - 1), total - largest - least * (number_of - 1)
    while surplus > 0:
        candidates = [i for i in range(1, number_of) if holding[i] < largest] or [i for i in range(1, number_of) if holding[i] < most]
        whole, remaining = sum([portions[i] for i in candidates]), surplus
        for i in candidates:
            addition = min(most - holding[i], max(1, remaining * portions[i] // whole), surplus)
            holding[i] = holding[i] + addition
            surplus = surplus - addition
    return np.array(holding)


def normal_values(rng, dims, scale, bound, cuts=(), held_as=jnp.bfloat16):
    gain = shard_levels(rng, dims, cuts, -0.22, 0.18) if cuts else 1.0
    entries = jax.random.normal(rng, dims, jnp.float32) * scale * gain
    return jnp.minimum(jnp.maximum(entries, -bound), bound).astype(held_as)


def setup_inputs(seed: int = 0) -> dict:
    arg_keys = jax.random.split(jax.random.key(seed), 9)
    queries = draw_queries(jax.random.fold_in(arg_keys[8], 71), 0)
    probe_groups_keys = jax.random.split(jax.random.fold_in(arg_keys[1], 1), QUERIES // Q_DEV)
    probe_groups_turns = jax.random.permutation(jax.random.fold_in(arg_keys[1], 3), QUERIES // Q_DEV)
    probe_groups = jax.vmap(lambda own, number: routed_block(jax.random.fold_in(arg_keys[1], 2), own, number, Q_DEV, N_CELL, 2, CAP, 2))(probe_groups_keys, probe_groups_turns).reshape((QUERIES, 2))
    probe_cells = draw_probe_cells(jax.random.fold_in(arg_keys[8], 71), 0)
    coarse = normal_values(arg_keys[3], (CELLS, DIM), 0.2, 1.1953125, ((0, 16), (1, 16)))
    codebooks = normal_values(arg_keys[4], (M, SD, K), 0.25, 1.5, ((0, 16),))
    codes = place_ends(jax.random.randint(arg_keys[5], (CELLS, M, ROWS), 0, K), jax.random.fold_in(arg_keys[5], 1), 0, K - 1).astype(jnp.int32)
    lengths = uneven_parts(arg_keys[6], CELLS, CELLS * ROWS // 2, ROWS, 2).astype(jnp.int32)
    payload = normal_values(arg_keys[7], (CELLS, ROWS, PW), 1.0, 6.0, ((0, 16), (1, 16)))
    return {"queries": queries, "probe_groups": probe_groups, "probe_cells": probe_cells, "coarse": coarse, "codebooks": codebooks, "codes": codes, "lengths": lengths, "payload": payload}


score_scale = 0.3
floor_score = -1.0e30


def decode_group(coarse_part, codebooks, codes_part):
    picked = jax.vmap(lambda book, index: book[:, index], in_axes=(0, 1))(codebooks, codes_part)
    recon = picked.reshape(DIM, CELL_DEV, ROWS).astype(jnp.float32)
    summed = recon + coarse_part.T.astype(jnp.float32)[:, :, None]
    return summed.astype(jnp.bfloat16).reshape(DIM, CELL_DEV * ROWS)


def reference(queries, probe_groups, probe_cells, coarse, codebooks, codes, lengths, payload):
    limit = N_CELL * CAP

    def one_group(group):
        start = group * CELL_DEV
        codes_part = lax.dynamic_slice_in_dim(codes, start, CELL_DEV, 0)
        coarse_part = lax.dynamic_slice_in_dim(coarse, start, CELL_DEV, 0)
        live_count = lax.dynamic_slice_in_dim(lengths, start, CELL_DEV, 0)
        table = lax.dynamic_slice_in_dim(payload, start, CELL_DEV, 0).reshape(CELL_DEV * ROWS, PW)
        decoded = decode_group(coarse_part, codebooks, codes_part)
        sq_norm = jnp.sum(jnp.square(decoded.astype(jnp.float32)), axis=0)
        hit = probe_groups == group
        routed = jnp.any(hit, axis=1)
        order = jnp.argsort(1 - routed.astype(jnp.int32), stable=True)[:limit].astype(jnp.int32)
        valid = routed[order]
        route = hit[order, 1].astype(jnp.int32)
        cells = probe_cells[order, route]
        probed = jnp.any(cells[:, :, None] == jnp.arange(CELL_DEV, dtype=jnp.int32)[None, None, :], axis=1)
        live = jnp.arange(ROWS, dtype=jnp.int32)[None, :] < live_count[:, None]
        keep = (probed[:, :, None] & live[None, :, :]).reshape(limit, CELL_DEV * ROWS)
        raw = jnp.dot(queries[order], decoded, preferred_element_type=jnp.float32)
        values = (raw - 0.5 * sq_norm[None, :]) * score_scale
        peak = jnp.max(jnp.where(keep, values, floor_score), axis=1)
        weights = jnp.where(keep, jnp.exp(values - peak[:, None]), 0.0).astype(jnp.bfloat16)
        mass = jnp.sum(weights.astype(jnp.float32), axis=1)
        part = jnp.dot(weights, table, preferred_element_type=jnp.float32)
        target = jnp.where(valid, order, QUERIES).astype(jnp.int32)
        return target, route, peak, mass, part

    target, route, peak, mass, part = lax.map(one_group, jnp.arange(N_CELL, dtype=jnp.int32))
    target = target.reshape(-1)
    route = route.reshape(-1)
    peaks = jnp.full((QUERIES, 2), floor_score, jnp.float32).at[target, route].set(peak.reshape(-1), mode="drop")
    masses = jnp.zeros((QUERIES, 2), jnp.float32).at[target, route].set(mass.reshape(-1), mode="drop")
    parts = jnp.zeros((QUERIES, 2, PW), jnp.float32).at[target, route].set(part.reshape(-1, PW), mode="drop")
    top = jnp.max(peaks, axis=1, keepdims=True)
    scale = jnp.exp(peaks - top)
    upper = jnp.sum(scale[:, :, None] * parts, axis=1)
    lower = jnp.sum(scale * masses, axis=1)
    return (upper / lower[:, None]).astype(jnp.bfloat16)
```

```python
import jax
import jax.numpy as jnp
from jax import lax
from jax.sharding import PartitionSpec as P

CAP = 64


score_scale = 0.3
floor_score = -1e30


def slot_table(probe_groups, groups, capacity):
    marks = (probe_groups[:, :, None] == jnp.arange(groups, dtype=jnp.int32)[None, None, :]).astype(
        jnp.int32
    )
    routed = jnp.sum(marks, axis=1)
    earlier = jnp.cumsum(routed, axis=0) - routed
    position = jnp.sum(marks * earlier[:, None, :], axis=2)
    return probe_groups * capacity + position


def pack_slots(rows, probe_cells, slots, total):
    flat = slots.reshape(-1)
    doubled = jnp.repeat(rows, 2, axis=0)
    buffer = jnp.zeros((total, rows.shape[1]), rows.dtype).at[flat].set(doubled)
    named = probe_cells.reshape(flat.shape[0], -1).astype(jnp.bfloat16)
    cell_marks = jnp.full((total, probe_cells.shape[2]), -1.0, jnp.bfloat16).at[flat].set(named)
    return (buffer, cell_marks)


def decode(coarse, codebooks, codes, parts):
    cell_count, sub_count, row_count = codes.shape
    width = codebooks.shape[1]
    rows_part = row_count // parts
    grouped = codes.reshape(cell_count, sub_count, parts, rows_part)
    grouped = jnp.transpose(grouped, (2, 1, 0, 3)).reshape(parts, sub_count, cell_count * rows_part)
    centroid_ids = jnp.arange(codebooks.shape[2], dtype=jnp.int32)
    onehot = (grouped[..., None] == centroid_ids).astype(jnp.bfloat16)
    books = jnp.broadcast_to(codebooks[None], (parts,) + codebooks.shape)
    picked = lax.dot_general(
        books, onehot, (((3,), (3,)), ((0, 1), (0, 1))), preferred_element_type=jnp.float32
    )
    picked = picked.reshape(parts, sub_count * width, cell_count, rows_part)
    recon = picked + coarse.T.astype(jnp.float32)[None, :, :, None]
    return recon.astype(jnp.bfloat16).reshape(parts, sub_count * width, cell_count * rows_part)


def local(queries, probe_groups, probe_cells, coarse, codebooks, codes, lengths, payload):
    groups = lax.axis_size("cell")
    parts = lax.axis_size("sub")
    capacity = CAP
    total = groups * capacity
    cell_dev = codes.shape[0]
    pw = payload.shape[2]
    chunk = pw // parts

    local_vectors = decode(coarse, codebooks, codes, parts)
    decoded = lax.all_to_all(local_vectors, "sub", split_axis=0, concat_axis=0, tiled=True)
    decoded = decoded.reshape(-1, decoded.shape[2])

    slots = slot_table(probe_groups, groups, capacity)
    buffer, cell_marks = pack_slots(queries, probe_cells, slots, total)
    arrived = lax.all_to_all(
        buffer.reshape(groups, capacity, -1), "cell", split_axis=0, concat_axis=0, tiled=True
    )
    arrived_cells = lax.all_to_all(
        cell_marks.reshape(groups, capacity, -1), "cell", split_axis=0, concat_axis=0, tiled=True
    )
    full_rows = lax.all_gather(arrived.reshape(total, -1), "sub", axis=1, tiled=True)
    cell_ids = arrived_cells.reshape(total, -1).astype(jnp.int32)
    probed = jnp.any(
        cell_ids[:, :, None] == jnp.arange(cell_dev, dtype=jnp.int32)[None, None, :], axis=1
    )

    row_local = payload.shape[1]
    sq_norm = jnp.sum(jnp.square(decoded.astype(jnp.float32)), axis=0)
    first_row = lax.axis_index("sub") * row_local
    live = (first_row + jnp.arange(row_local, dtype=jnp.int32))[None, :] < lengths[:, None]
    keep = (probed[:, :, None] & live[None, :, :]).reshape(total, -1)
    table = payload.reshape(-1, pw)

    raw = jnp.dot(full_rows, decoded, preferred_element_type=jnp.float32)
    values = (raw - 0.5 * sq_norm[None, :]) * score_scale
    local_peak = jnp.max(jnp.where(keep, values, floor_score), axis=1)
    peak = jnp.max(lax.all_gather(local_peak, "sub", axis=0), axis=0)

    weights = jnp.where(keep, jnp.exp(values - peak[:, None]), 0.0).astype(jnp.bfloat16)
    mass = jnp.sum(weights.astype(jnp.float32), axis=1)
    part_t = lax.dot_general(
        table, weights, (((0,), (1,)), ((), ())), preferred_element_type=jnp.float32
    )
    sendable = jnp.concatenate(
        [
            part_t.reshape(parts, chunk, total),
            jnp.broadcast_to(mass[None, None, :], (parts, 1, total)),
        ],
        axis=1,
    )
    pieces = lax.all_to_all(sendable, "sub", split_axis=0, concat_axis=0, tiled=True)
    reduced = jnp.sum(pieces, axis=0)
    outgoing = jnp.concatenate([reduced, peak[None, :]], axis=0)
    back = lax.all_to_all(
        outgoing.reshape(chunk + 2, groups, capacity), "cell", split_axis=1, concat_axis=1, tiled=True
    )
    back = back.reshape(chunk + 2, total)
    picked = back[:, slots]
    parts_back = picked[:chunk]
    masses = picked[chunk]
    peaks = picked[chunk + 1]
    top = jnp.max(peaks, axis=1, keepdims=True)
    scale = jnp.exp(peaks - top)
    upper = jnp.sum(scale[None, :, :] * parts_back, axis=2)
    lower = jnp.sum(scale * masses, axis=1)
    pooled = (upper / lower[None, :]).astype(jnp.bfloat16)
    return lax.all_gather(pooled, "sub", axis=0, tiled=True).T


def solution(mesh):
    placed = (
        P("cell", "sub"),
        P("cell", None),
        P("cell", None, None),
        P("cell", "sub"),
        P("sub", None, None),
        P("cell", "sub", None),
        P("cell"),
        P("cell", "sub", None),
    )
    return jax.shard_map(
        local, mesh=mesh, in_specs=placed, out_specs=P("cell", None), check_vma=False
    )
```

```python
import jax
import jax.numpy as jnp
from jax import lax
from jax.sharding import PartitionSpec as P

CAP = 64


score_scale = 0.3
floor_score = -1e30


def slot_table(probe_groups, groups, capacity):
    marks = (probe_groups[:, :, None] == jnp.arange(groups, dtype=jnp.int32)[None, None, :]).astype(
        jnp.int32
    )
    routed = jnp.sum(marks, axis=1)
    earlier = jnp.cumsum(routed, axis=0) - routed
    position = jnp.sum(marks * earlier[:, None, :], axis=2)
    return probe_groups * capacity + position


def pack_slots(rows, probe_cells, slots, total):
    flat = slots.reshape(-1)
    doubled = jnp.repeat(rows, 2, axis=0)
    buffer = jnp.zeros((total, rows.shape[1]), rows.dtype).at[flat].set(doubled)
    named = probe_cells.reshape(flat.shape[0], -1).astype(jnp.bfloat16)
    cell_marks = jnp.full((total, probe_cells.shape[2]), -1.0, jnp.bfloat16).at[flat].set(named)
    return (buffer, cell_marks)


def decode(coarse, codebooks, codes, parts):
    cell_count, sub_count, row_count = codes.shape
    width = codebooks.shape[1]
    rows_part = row_count // parts
    grouped = codes.reshape(cell_count, sub_count, parts, rows_part)
    grouped = jnp.transpose(grouped, (2, 1, 0, 3)).reshape(parts, sub_count, cell_count * rows_part)
    centroid_ids = jnp.arange(codebooks.shape[2], dtype=jnp.int32)
    onehot = (grouped[..., None] == centroid_ids).astype(jnp.bfloat16)
    books = jnp.broadcast_to(codebooks[None], (parts,) + codebooks.shape)
    picked = lax.dot_general(
        books, onehot, (((3,), (3,)), ((0, 1), (0, 1))), preferred_element_type=jnp.float32
    )
    picked = picked.reshape(parts, sub_count * width, cell_count, rows_part)
    recon = picked + coarse.T.astype(jnp.float32)[None, :, :, None]
    return recon.astype(jnp.bfloat16).reshape(parts, sub_count * width, cell_count * rows_part)


def gather_by_exchange(x, axis):
    count = lax.axis_size(axis)
    copies = jnp.broadcast_to(x[None], (count,) + x.shape)
    return lax.all_to_all(copies, axis, split_axis=0, concat_axis=0, tiled=True)


def local(queries, probe_groups, probe_cells, coarse, codebooks, codes, lengths, payload):
    groups = lax.axis_size("cell")
    parts = lax.axis_size("sub")
    capacity = CAP
    total = groups * capacity
    cell_dev = codes.shape[0]
    pw = payload.shape[2]
    chunk = pw // parts

    local_vectors = decode(coarse, codebooks, codes, parts)
    decoded = lax.all_to_all(local_vectors, "sub", split_axis=0, concat_axis=0, tiled=True)
    decoded = decoded.reshape(-1, decoded.shape[2])

    slots = slot_table(probe_groups, groups, capacity)
    buffer, cell_marks = pack_slots(queries, probe_cells, slots, total)
    arrived = lax.all_to_all(
        buffer.reshape(groups, capacity, -1), "cell", split_axis=0, concat_axis=0, tiled=True
    )
    arrived_cells = lax.all_to_all(
        cell_marks.reshape(groups, capacity, -1), "cell", split_axis=0, concat_axis=0, tiled=True
    )
    query_parts = gather_by_exchange(arrived.reshape(total, -1), "sub")
    cell_ids = arrived_cells.reshape(total, -1).astype(jnp.int32)
    probed = jnp.any(
        cell_ids[:, :, None] == jnp.arange(cell_dev, dtype=jnp.int32)[None, None, :], axis=1
    )

    row_local = payload.shape[1]
    sq_norm = jnp.sum(jnp.square(decoded.astype(jnp.float32)), axis=0)
    first_row = lax.axis_index("sub") * row_local
    live = (first_row + jnp.arange(row_local, dtype=jnp.int32))[None, :] < lengths[:, None]
    keep = (probed[:, :, None] & live[None, :, :]).reshape(total, -1)
    table = payload.reshape(-1, pw)

    raw = jnp.einsum(
        "sqd,sdr->qr",
        query_parts,
        decoded.reshape(parts, -1, decoded.shape[1]),
        preferred_element_type=jnp.float32,
    )
    values = (raw - 0.5 * sq_norm[None, :]) * score_scale
    local_peak = jnp.max(jnp.where(keep, values, floor_score), axis=1)
    peak = jnp.max(gather_by_exchange(local_peak, "sub"), axis=0)

    weights = jnp.where(keep, jnp.exp(values - peak[:, None]), 0.0).astype(jnp.bfloat16)
    mass = jnp.sum(weights.astype(jnp.float32), axis=1)
    part_t = lax.dot_general(
        table, weights, (((0,), (1,)), ((), ())), preferred_element_type=jnp.float32
    )
    sendable = jnp.concatenate(
        [
            part_t.reshape(parts, chunk, total),
            jnp.broadcast_to(mass[None, None, :], (parts, 1, total)),
        ],
        axis=1,
    )
    pieces = lax.all_to_all(sendable, "sub", split_axis=0, concat_axis=0, tiled=True)
    reduced = jnp.sum(pieces, axis=0)
    outgoing = jnp.concatenate([reduced, peak[None, :]], axis=0)
    back = lax.all_to_all(
        outgoing.reshape(chunk + 2, groups, capacity), "cell", split_axis=1, concat_axis=1, tiled=True
    )
    back = back.reshape(chunk + 2, total)
    picked = back[:, slots]
    parts_back = picked[:chunk]
    masses = picked[chunk]
    peaks = picked[chunk + 1]
    top = jnp.max(peaks, axis=1, keepdims=True)
    scale = jnp.exp(peaks - top)
    upper = jnp.sum(scale[None, :, :] * parts_back, axis=2)
    lower = jnp.sum(scale * masses, axis=1)
    pooled = (upper / lower[None, :]).astype(jnp.bfloat16)
    return gather_by_exchange(pooled, "sub").reshape(pw, -1).T


def solution(mesh):
    placed = (
        P("cell", "sub"),
        P("cell", None),
        P("cell", None, None),
        P("cell", "sub"),
        P("sub", None, None),
        P("cell", "sub", None),
        P("cell"),
        P("cell", "sub", None),
    )
    return jax.shard_map(
        local, mesh=mesh, in_specs=placed, out_specs=P("cell", None), check_vma=False
    )
```

```python
import jax
import jax.numpy as jnp
from jax import lax
from jax.sharding import PartitionSpec as P

CAP = 64


score_scale = 0.3
floor_score = -1e30


def slot_table(probe_groups, groups, capacity):
    marks = (probe_groups[:, :, None] == jnp.arange(groups, dtype=jnp.int32)[None, None, :]).astype(
        jnp.int32
    )
    routed = jnp.sum(marks, axis=1)
    earlier = jnp.cumsum(routed, axis=0) - routed
    position = jnp.sum(marks * earlier[:, None, :], axis=2)
    return probe_groups * capacity + position


def pack_slots(rows, probe_cells, slots, total):
    flat = slots.reshape(-1)
    doubled = jnp.repeat(rows, 2, axis=0)
    buffer = jnp.zeros((total, rows.shape[1]), rows.dtype).at[flat].set(doubled)
    named = probe_cells.reshape(flat.shape[0], -1).astype(jnp.bfloat16)
    cell_marks = jnp.full((total, probe_cells.shape[2]), -1.0, jnp.bfloat16).at[flat].set(named)
    return (buffer, cell_marks)


def decode(coarse, codebooks, codes, parts):
    cell_count, sub_count, row_count = codes.shape
    width = codebooks.shape[1]
    rows_part = row_count // parts
    grouped = codes.reshape(cell_count, sub_count, parts, rows_part)
    grouped = jnp.transpose(grouped, (2, 1, 0, 3)).reshape(parts, sub_count, cell_count * rows_part)
    centroid_ids = jnp.arange(codebooks.shape[2], dtype=jnp.int32)
    onehot = (grouped[..., None] == centroid_ids).astype(jnp.bfloat16)
    books = jnp.broadcast_to(codebooks[None], (parts,) + codebooks.shape)
    picked = lax.dot_general(
        books, onehot, (((3,), (3,)), ((0, 1), (0, 1))), preferred_element_type=jnp.float32
    )
    picked = picked.reshape(parts, sub_count * width, cell_count, rows_part)
    recon = picked + coarse.T.astype(jnp.float32)[None, :, :, None]
    return recon.astype(jnp.bfloat16).reshape(parts, sub_count * width, cell_count * rows_part)


def gather_by_exchange(x, axis):
    count = lax.axis_size(axis)
    copies = jnp.broadcast_to(x[None], (count,) + x.shape)
    return lax.all_to_all(copies, axis, split_axis=0, concat_axis=0, tiled=True)


def local(queries, probe_groups, probe_cells, coarse, codebooks, codes, lengths, payload):
    groups = lax.axis_size("cell")
    parts = lax.axis_size("sub")
    capacity = CAP
    total = groups * capacity
    cell_dev = codes.shape[0]
    pw = payload.shape[2]
    chunk = pw // parts

    local_vectors = decode(coarse, codebooks, codes, parts)

    slots = slot_table(probe_groups, groups, capacity)
    buffer, cell_marks = pack_slots(queries, probe_cells, slots, total)
    arrived = lax.all_to_all(
        buffer.reshape(groups, capacity, -1), "cell", split_axis=0, concat_axis=0, tiled=True
    )
    arrived_cells = lax.all_to_all(
        cell_marks.reshape(groups, capacity, -1), "cell", split_axis=0, concat_axis=0, tiled=True
    )
    query_cols = jnp.broadcast_to(arrived.reshape(total, -1).T[None], (parts,) + (arrived.shape[2], total))
    exchanged = lax.all_to_all(
        jnp.concatenate([local_vectors, query_cols], axis=2), "sub", split_axis=0, concat_axis=0, tiled=True
    )
    row_cols = local_vectors.shape[2]
    decoded_parts = exchanged[:, :, :row_cols]
    query_parts = exchanged[:, :, row_cols:]
    decoded = decoded_parts.reshape(-1, row_cols)
    cell_ids = arrived_cells.reshape(total, -1).astype(jnp.int32)
    probed = jnp.any(
        cell_ids[:, :, None] == jnp.arange(cell_dev, dtype=jnp.int32)[None, None, :], axis=1
    )

    row_local = payload.shape[1]
    sq_norm = jnp.sum(jnp.square(decoded.astype(jnp.float32)), axis=0)
    first_row = lax.axis_index("sub") * row_local
    live = (first_row + jnp.arange(row_local, dtype=jnp.int32))[None, :] < lengths[:, None]
    keep = (probed[:, :, None] & live[None, :, :]).reshape(total, -1)
    table = payload.reshape(-1, pw)

    raw = jnp.einsum("sdq,sdr->qr", query_parts, decoded_parts, preferred_element_type=jnp.float32)
    values = (raw - 0.5 * sq_norm[None, :]) * score_scale
    local_peak = jnp.max(jnp.where(keep, values, floor_score), axis=1)
    peak = jnp.max(gather_by_exchange(local_peak, "sub"), axis=0)

    weights = jnp.where(keep, jnp.exp(values - peak[:, None]), 0.0).astype(jnp.bfloat16)
    mass = jnp.sum(weights.astype(jnp.float32), axis=1)
    part_t = lax.dot_general(
        table, weights, (((0,), (1,)), ((), ())), preferred_element_type=jnp.float32
    )
    sendable = jnp.concatenate(
        [
            part_t.reshape(parts, chunk, total),
            jnp.broadcast_to(mass[None, None, :], (parts, 1, total)),
        ],
        axis=1,
    )
    pieces = lax.all_to_all(sendable, "sub", split_axis=0, concat_axis=0, tiled=True)
    reduced = jnp.sum(pieces, axis=0)
    outgoing = jnp.concatenate([reduced, peak[None, :]], axis=0)
    back = lax.all_to_all(
        outgoing.reshape(chunk + 2, groups, capacity), "cell", split_axis=1, concat_axis=1, tiled=True
    )
    back = back.reshape(chunk + 2, total)
    picked = back[:, slots]
    parts_back = picked[:chunk]
    masses = picked[chunk]
    peaks = picked[chunk + 1]
    top = jnp.max(peaks, axis=1, keepdims=True)
    scale = jnp.exp(peaks - top)
    upper = jnp.sum(scale[None, :, :] * parts_back, axis=2)
    lower = jnp.sum(scale * masses, axis=1)
    pooled = (upper / lower[None, :]).astype(jnp.bfloat16)
    return gather_by_exchange(pooled, "sub").reshape(pw, -1).T


def solution(mesh):
    placed = (
        P("cell", "sub"),
        P("cell", None),
        P("cell", None, None),
        P("cell", "sub"),
        P("sub", None, None),
        P("cell", "sub", None),
        P("cell"),
        P("cell", "sub", None),
    )
    return jax.shard_map(
        local, mesh=mesh, in_specs=placed, out_specs=P("cell", None), check_vma=False
    )
```

```python
import jax
import jax.numpy as jnp
from jax import lax
from jax.experimental import pallas as pl
from jax.sharding import PartitionSpec as P

CAP = 64


score_scale = 0.3
floor_score = -1e30


def slot_table(probe_groups, groups, capacity):
    marks = (probe_groups[:, :, None] == jnp.arange(groups, dtype=jnp.int32)[None, None, :]).astype(
        jnp.int32
    )
    routed = jnp.sum(marks, axis=1)
    earlier = jnp.cumsum(routed, axis=0) - routed
    position = jnp.sum(marks * earlier[:, None, :], axis=2)
    return probe_groups * capacity + position


def pack_slots(rows, probe_cells, slots, total):
    flat = slots.reshape(-1)
    doubled = jnp.repeat(rows, 2, axis=0)
    buffer = jnp.zeros((total, rows.shape[1]), rows.dtype).at[flat].set(doubled)
    named = probe_cells.reshape(flat.shape[0], -1).astype(jnp.bfloat16)
    cell_marks = jnp.full((total, probe_cells.shape[2]), -1.0, jnp.bfloat16).at[flat].set(named)
    return (buffer, cell_marks)


def decode_kernel(codes_ref, book_ref, base_ref, out_ref):
    m_count, width, k_count = book_ref.shape
    n = codes_ref.shape[2]
    ids = lax.broadcasted_iota(jnp.int32, (k_count, n), 0)
    for m in range(m_count):
        row = codes_ref[0, m : m + 1, :]
        onehot = (ids == row).astype(jnp.bfloat16)
        val = jnp.dot(book_ref[m], onehot, preferred_element_type=jnp.float32)
        base = base_ref[m * width : (m + 1) * width, :].astype(jnp.float32)
        out_ref[0, m * width : (m + 1) * width, :] = (val + base).astype(jnp.bfloat16)


def decode(base, codebooks, codes_blocks):
    blocks, per_block, n = codes_blocks.shape
    width, k_count = codebooks.shape[1], codebooks.shape[2]
    return pl.pallas_call(
        decode_kernel,
        grid=(blocks,),
        in_specs=[
            pl.BlockSpec((1, per_block, n), lambda p: (p, 0, 0)),
            pl.BlockSpec((per_block, width, k_count), lambda p: (p, 0, 0)),
            pl.BlockSpec((per_block * width, n), lambda p: (p, 0)),
        ],
        out_specs=pl.BlockSpec((1, per_block * width, n), lambda p: (p, 0, 0)),
        out_shape=jax.ShapeDtypeStruct((blocks, per_block * width, n), jnp.bfloat16),
    )(codes_blocks, codebooks, base)


def gather_by_exchange(x, axis):
    count = lax.axis_size(axis)
    copies = jnp.broadcast_to(x[None], (count,) + x.shape)
    return lax.all_to_all(copies, axis, split_axis=0, concat_axis=0, tiled=True)


def local(queries, probe_groups, probe_cells, coarse, codebooks, codes, lengths, payload):
    groups = lax.axis_size("cell")
    parts = lax.axis_size("sub")
    capacity = CAP
    total = groups * capacity
    cell_dev = codes.shape[0]
    pw = payload.shape[2]
    chunk = pw // parts

    cell_count, sub_count, row_count = codes.shape
    rows_part = row_count // parts
    own_codes = codes.reshape(cell_count, sub_count, parts, rows_part)
    own_codes = jnp.transpose(own_codes, (2, 0, 1, 3)).astype(jnp.bfloat16).reshape(parts, -1)
    tables = jnp.concatenate(
        [
            own_codes,
            jnp.broadcast_to(codebooks.reshape(1, -1), (parts, codebooks.size)),
            jnp.broadcast_to(coarse.reshape(1, -1), (parts, coarse.size)),
        ],
        axis=1,
    )
    tables = lax.all_to_all(tables, "sub", split_axis=0, concat_axis=0, tiled=True)
    code_size = own_codes.shape[1]
    book_size = codebooks.size
    got_codes = tables[:, :code_size].reshape(parts, cell_count, sub_count, rows_part)
    got_codes = jnp.transpose(got_codes, (0, 2, 1, 3)).astype(jnp.int32)
    got_codes = got_codes.reshape(parts, sub_count, cell_count * rows_part)
    all_books = tables[:, code_size : code_size + book_size].reshape((-1,) + codebooks.shape[1:])
    all_coarse = tables[:, code_size + book_size :].reshape(parts, cell_count, -1)
    all_coarse = jnp.transpose(all_coarse, (1, 0, 2)).reshape(cell_count, -1)
    base = jnp.repeat(all_coarse.T, rows_part, axis=1)
    decoded_parts = decode(base, all_books, got_codes)

    slots = slot_table(probe_groups, groups, capacity)
    buffer, cell_marks = pack_slots(queries, probe_cells, slots, total)
    arrived = lax.all_to_all(
        buffer.reshape(groups, capacity, -1), "cell", split_axis=0, concat_axis=0, tiled=True
    )
    arrived_cells = lax.all_to_all(
        cell_marks.reshape(groups, capacity, -1), "cell", split_axis=0, concat_axis=0, tiled=True
    )
    query_parts = gather_by_exchange(arrived.reshape(total, -1).T, "sub")
    decoded = decoded_parts.reshape(-1, decoded_parts.shape[2])
    cell_ids = arrived_cells.reshape(total, -1).astype(jnp.int32)
    probed = jnp.any(
        cell_ids[:, :, None] == jnp.arange(cell_dev, dtype=jnp.int32)[None, None, :], axis=1
    )

    row_local = payload.shape[1]
    sq_norm = jnp.sum(jnp.square(decoded.astype(jnp.float32)), axis=0)
    first_row = lax.axis_index("sub") * row_local
    live = (first_row + jnp.arange(row_local, dtype=jnp.int32))[None, :] < lengths[:, None]
    keep = (probed[:, :, None] & live[None, :, :]).reshape(total, -1)
    table = payload.reshape(-1, pw)

    raw = jnp.einsum("sdq,sdr->qr", query_parts, decoded_parts, preferred_element_type=jnp.float32)
    values = (raw - 0.5 * sq_norm[None, :]) * score_scale
    local_peak = jnp.max(jnp.where(keep, values, floor_score), axis=1)
    peak = jnp.max(gather_by_exchange(local_peak, "sub"), axis=0)

    weights = jnp.where(keep, jnp.exp(values - peak[:, None]), 0.0).astype(jnp.bfloat16)
    mass = jnp.sum(weights.astype(jnp.float32), axis=1)
    part_t = lax.dot_general(
        table, weights, (((0,), (1,)), ((), ())), preferred_element_type=jnp.float32
    )
    sendable = jnp.concatenate(
        [
            part_t.reshape(parts, chunk, total),
            jnp.broadcast_to(mass[None, None, :], (parts, 1, total)),
        ],
        axis=1,
    )
    pieces = lax.all_to_all(sendable, "sub", split_axis=0, concat_axis=0, tiled=True)
    reduced = jnp.sum(pieces, axis=0)
    outgoing = jnp.concatenate([reduced, peak[None, :]], axis=0)
    back = lax.all_to_all(
        outgoing.reshape(chunk + 2, groups, capacity), "cell", split_axis=1, concat_axis=1, tiled=True
    )
    back = back.reshape(chunk + 2, total)
    picked = back[:, slots]
    parts_back = picked[:chunk]
    masses = picked[chunk]
    peaks = picked[chunk + 1]
    top = jnp.max(peaks, axis=1, keepdims=True)
    scale = jnp.exp(peaks - top)
    upper = jnp.sum(scale[None, :, :] * parts_back, axis=2)
    lower = jnp.sum(scale * masses, axis=1)
    pooled = (upper / lower[None, :]).astype(jnp.bfloat16)
    return gather_by_exchange(pooled, "sub").reshape(pw, -1).T


def solution(mesh):
    placed = (
        P("cell", "sub"),
        P("cell", None),
        P("cell", None, None),
        P("cell", "sub"),
        P("sub", None, None),
        P("cell", "sub", None),
        P("cell"),
        P("cell", "sub", None),
    )
    return jax.shard_map(
        local, mesh=mesh, in_specs=placed, out_specs=P("cell", None), check_vma=False
    )
```

```python
import jax
import jax.numpy as jnp
from jax import lax
from jax.experimental import pallas as pl
from jax.sharding import PartitionSpec as P


CAP = 64


score_scale = 0.3
floor_score = -1e30


def slot_table(probe_groups, groups, capacity):
    marks = (probe_groups[:, :, None] == jnp.arange(groups, dtype=jnp.int32)[None, None, :]).astype(
        jnp.int32
    )
    routed = jnp.sum(marks, axis=1)
    earlier = jnp.cumsum(routed, axis=0) - routed
    position = jnp.sum(marks * earlier[:, None, :], axis=2)
    return probe_groups * capacity + position


def pack_slots(rows, probe_cells, slots, total):
    flat = slots.reshape(-1)
    doubled = jnp.repeat(rows, 2, axis=0)
    buffer = jnp.zeros((total, rows.shape[1]), rows.dtype).at[flat].set(doubled)
    named = probe_cells.reshape(flat.shape[0], -1).astype(jnp.bfloat16)
    cell_marks = jnp.full((total, probe_cells.shape[2]), -1.0, jnp.bfloat16).at[flat].set(named)
    return (buffer, cell_marks)


def decode_kernel(codes_ref, book_ref, base_ref, out_ref):
    m_count, width, k_count = book_ref.shape
    n = codes_ref.shape[2]
    ids = lax.broadcasted_iota(jnp.int32, (k_count, n), 0)
    for m in range(m_count):
        row = codes_ref[0, m : m + 1, :]
        onehot = (ids == row).astype(jnp.bfloat16)
        val = jnp.dot(book_ref[m], onehot, preferred_element_type=jnp.float32)
        base = base_ref[m * width : (m + 1) * width, :].astype(jnp.float32)
        out_ref[0, m * width : (m + 1) * width, :] = (val + base).astype(jnp.bfloat16)


def decode(base, codebooks, codes_blocks):
    blocks, per_block, n = codes_blocks.shape
    width, k_count = codebooks.shape[1], codebooks.shape[2]
    return pl.pallas_call(
        decode_kernel,
        grid=(blocks,),
        in_specs=[
            pl.BlockSpec((1, per_block, n), lambda p: (p, 0, 0)),
            pl.BlockSpec((per_block, width, k_count), lambda p: (p, 0, 0)),
            pl.BlockSpec((per_block * width, n), lambda p: (p, 0)),
        ],
        out_specs=pl.BlockSpec((1, per_block * width, n), lambda p: (p, 0, 0)),
        out_shape=jax.ShapeDtypeStruct((blocks, per_block * width, n), jnp.bfloat16),
    )(codes_blocks, codebooks, base)


def gather_by_exchange(x, axis):
    count = lax.axis_size(axis)
    copies = jnp.broadcast_to(x[None], (count,) + x.shape)
    return lax.all_to_all(copies, axis, split_axis=0, concat_axis=0, tiled=True)


def local(queries, probe_groups, probe_cells, coarse, codebooks, codes, lengths, payload):
    groups = lax.axis_size("cell")
    parts = lax.axis_size("sub")
    capacity = CAP
    total = groups * capacity
    cell_dev = codes.shape[0]
    pw = payload.shape[2]
    chunk = pw // parts

    cell_count, sub_count, row_count = codes.shape
    rows_part = row_count // parts
    own_codes = codes.reshape(cell_count, sub_count, parts, rows_part)
    own_codes = jnp.transpose(own_codes, (2, 0, 1, 3)).astype(jnp.bfloat16).reshape(parts, -1)
    tables = jnp.concatenate(
        [
            own_codes,
            jnp.broadcast_to(codebooks.reshape(1, -1), (parts, codebooks.size)),
            jnp.broadcast_to(coarse.reshape(1, -1), (parts, coarse.size)),
        ],
        axis=1,
    )
    tables = lax.all_to_all(tables, "sub", split_axis=0, concat_axis=0, tiled=True)
    code_size = own_codes.shape[1]
    book_size = codebooks.size
    got_codes = tables[:, :code_size].reshape(parts, cell_count, sub_count, rows_part)
    got_codes = jnp.transpose(got_codes, (0, 2, 1, 3)).astype(jnp.int32)
    got_codes = got_codes.reshape(parts, sub_count, cell_count * rows_part)
    all_books = tables[:, code_size : code_size + book_size].reshape((-1,) + codebooks.shape[1:])
    all_coarse = tables[:, code_size + book_size :].reshape(parts, cell_count, -1)
    all_coarse = jnp.transpose(all_coarse, (1, 0, 2)).reshape(cell_count, -1)
    base = jnp.repeat(all_coarse.T, rows_part, axis=1)
    decoded_parts = decode(base, all_books, got_codes)

    slots = slot_table(probe_groups, groups, capacity)
    buffer, cell_marks = pack_slots(queries, probe_cells, slots, total)
    width = buffer.shape[1]
    arrived_all = lax.all_to_all(
        jnp.concatenate([buffer, cell_marks], axis=1).reshape(groups, capacity, -1),
        "cell",
        split_axis=0,
        concat_axis=0,
        tiled=True,
    ).reshape(total, -1)
    arrived = arrived_all[:, :width]
    arrived_cells = arrived_all[:, width:]
    query_parts = gather_by_exchange(arrived.T, "sub")
    decoded = decoded_parts.reshape(-1, decoded_parts.shape[2])
    cell_ids = arrived_cells.astype(jnp.int32)
    probed = jnp.any(
        cell_ids[:, :, None] == jnp.arange(cell_dev, dtype=jnp.int32)[None, None, :], axis=1
    )

    row_local = payload.shape[1]
    sq_norm = jnp.sum(jnp.square(decoded.astype(jnp.float32)), axis=0)
    first_row = lax.axis_index("sub") * row_local
    live = (first_row + jnp.arange(row_local, dtype=jnp.int32))[None, :] < lengths[:, None]
    keep = (probed[:, :, None] & live[None, :, :]).reshape(total, -1)
    table = payload.reshape(-1, pw)

    raw = jnp.einsum("sdq,sdr->qr", query_parts, decoded_parts, preferred_element_type=jnp.float32)
    values = (raw - 0.5 * sq_norm[None, :]) * score_scale
    local_peak = jnp.max(jnp.where(keep, values, floor_score), axis=1)
    peak = jnp.max(gather_by_exchange(local_peak, "sub"), axis=0)

    weights = jnp.where(keep, jnp.exp(values - peak[:, None]), 0.0).astype(jnp.bfloat16)
    mass = jnp.sum(weights.astype(jnp.float32), axis=1)
    part_t = lax.dot_general(
        table, weights, (((0,), (1,)), ((), ())), preferred_element_type=jnp.float32
    )
    sendable = jnp.concatenate(
        [
            part_t.reshape(parts, chunk, total),
            jnp.broadcast_to(mass[None, None, :], (parts, 1, total)),
        ],
        axis=1,
    )
    pieces = lax.all_to_all(sendable, "sub", split_axis=0, concat_axis=0, tiled=True)
    reduced = jnp.sum(pieces, axis=0)
    outgoing = jnp.concatenate([reduced, peak[None, :]], axis=0)
    back = lax.all_to_all(
        outgoing.reshape(chunk + 2, groups, capacity), "cell", split_axis=1, concat_axis=1, tiled=True
    )
    back = back.reshape(chunk + 2, total)
    picked = back[:, slots]
    parts_back = picked[:chunk]
    masses = picked[chunk]
    peaks = picked[chunk + 1]
    top = jnp.max(peaks, axis=1, keepdims=True)
    scale = jnp.exp(peaks - top)
    upper = jnp.sum(scale[None, :, :] * parts_back, axis=2)
    lower = jnp.sum(scale * masses, axis=1)
    pooled = (upper / lower[None, :]).astype(jnp.bfloat16)
    return gather_by_exchange(pooled, "sub").reshape(pw, -1).T


def solution(mesh):
    placed = (
        P("cell", "sub"),
        P("cell", None),
        P("cell", None, None),
        P("cell", "sub"),
        P("sub", None, None),
        P("cell", "sub", None),
        P("cell"),
        P("cell", "sub", None),
    )
    return jax.shard_map(
        local, mesh=mesh, in_specs=placed, out_specs=P("cell", None), check_vma=False
    )
```

```python
import jax
import jax.numpy as jnp
from jax import lax
from jax.experimental import pallas as pl
from jax.sharding import PartitionSpec as P


CAP = 64


score_scale = 0.3
floor_score = -1e30


def slot_table(probe_groups, groups, capacity):
    marks = (probe_groups[:, :, None] == jnp.arange(groups, dtype=jnp.int32)[None, None, :]).astype(
        jnp.int32
    )
    routed = jnp.sum(marks, axis=1)
    earlier = jnp.cumsum(routed, axis=0) - routed
    position = jnp.sum(marks * earlier[:, None, :], axis=2)
    return probe_groups * capacity + position


def pack_slots(rows, probe_cells, slots, total):
    flat = slots.reshape(-1)
    doubled = jnp.repeat(rows, 2, axis=0)
    buffer = jnp.zeros((total, rows.shape[1]), rows.dtype).at[flat].set(doubled)
    named = probe_cells.reshape(flat.shape[0], -1).astype(jnp.bfloat16)
    cell_marks = jnp.full((total, probe_cells.shape[2]), -1.0, jnp.bfloat16).at[flat].set(named)
    return (buffer, cell_marks)


def decode_kernel(codes_ref, book_ref, base_ref, out_ref):
    m_count, width, k_count = book_ref.shape
    n = codes_ref.shape[2]
    ids = lax.broadcasted_iota(jnp.int32, (k_count, n), 0)
    for m in range(m_count):
        row = codes_ref[0, m : m + 1, :]
        onehot = (ids == row).astype(jnp.bfloat16)
        val = jnp.dot(book_ref[m], onehot, preferred_element_type=jnp.float32)
        base = base_ref[m * width : (m + 1) * width, :].astype(jnp.float32)
        out_ref[0, m * width : (m + 1) * width, :] = (val + base).astype(jnp.bfloat16)


def decode(base, codebooks, codes_blocks):
    blocks, per_block, n = codes_blocks.shape
    width, k_count = codebooks.shape[1], codebooks.shape[2]
    return pl.pallas_call(
        decode_kernel,
        grid=(blocks,),
        in_specs=[
            pl.BlockSpec((1, per_block, n), lambda p: (p, 0, 0)),
            pl.BlockSpec((per_block, width, k_count), lambda p: (p, 0, 0)),
            pl.BlockSpec((per_block * width, n), lambda p: (p, 0)),
        ],
        out_specs=pl.BlockSpec((1, per_block * width, n), lambda p: (p, 0, 0)),
        out_shape=jax.ShapeDtypeStruct((blocks, per_block * width, n), jnp.bfloat16),
    )(codes_blocks, codebooks, base)


def gather_by_exchange(x, axis):
    count = lax.axis_size(axis)
    copies = jnp.broadcast_to(x[None], (count,) + x.shape)
    return lax.all_to_all(copies, axis, split_axis=0, concat_axis=0, tiled=True)


def local(queries, probe_groups, probe_cells, coarse, codebooks, codes, lengths, payload):
    groups = lax.axis_size("cell")
    parts = lax.axis_size("sub")
    capacity = CAP
    total = groups * capacity
    cell_dev = codes.shape[0]
    pw = payload.shape[2]
    chunk = pw // parts

    cell_count, sub_count, row_count = codes.shape
    rows_part = row_count // parts
    own_codes = codes.reshape(cell_count, sub_count, parts, rows_part)
    own_codes = jnp.transpose(own_codes, (2, 0, 1, 3)).astype(jnp.bfloat16).reshape(parts, -1)
    tables = jnp.concatenate(
        [
            own_codes,
            jnp.broadcast_to(codebooks.reshape(1, -1), (parts, codebooks.size)),
            jnp.broadcast_to(coarse.reshape(1, -1), (parts, coarse.size)),
        ],
        axis=1,
    )
    tables = lax.all_to_all(tables, "sub", split_axis=0, concat_axis=0, tiled=True)
    code_size = own_codes.shape[1]
    book_size = codebooks.size
    got_codes = tables[:, :code_size].reshape(parts, cell_count, sub_count, rows_part)
    got_codes = jnp.transpose(got_codes, (0, 2, 1, 3)).astype(jnp.int32)
    got_codes = got_codes.reshape(parts, sub_count, cell_count * rows_part)
    all_books = tables[:, code_size : code_size + book_size].reshape((-1,) + codebooks.shape[1:])
    all_coarse = tables[:, code_size + book_size :].reshape(parts, cell_count, -1)
    all_coarse = jnp.transpose(all_coarse, (1, 0, 2)).reshape(cell_count, -1)
    base = jnp.repeat(all_coarse.T, rows_part, axis=1)
    decoded_parts = decode(base, all_books, got_codes)

    slots = slot_table(probe_groups, groups, capacity)
    buffer, cell_marks = pack_slots(queries, probe_cells, slots, total)
    width = buffer.shape[1]
    arrived_all = lax.all_to_all(
        jnp.concatenate([buffer, cell_marks], axis=1).reshape(groups, -1),
        "cell",
        split_axis=0,
        concat_axis=0,
        tiled=True,
    ).reshape(total, -1)
    arrived = arrived_all[:, :width]
    arrived_cells = arrived_all[:, width:]
    query_parts = gather_by_exchange(arrived.T, "sub")
    decoded = decoded_parts.reshape(-1, decoded_parts.shape[2])
    cell_ids = arrived_cells.astype(jnp.int32)
    probed = jnp.any(
        cell_ids[:, :, None] == jnp.arange(cell_dev, dtype=jnp.int32)[None, None, :], axis=1
    )

    row_local = payload.shape[1]
    sq_norm = jnp.sum(jnp.square(decoded.astype(jnp.float32)), axis=0)
    first_row = lax.axis_index("sub") * row_local
    live = (first_row + jnp.arange(row_local, dtype=jnp.int32))[None, :] < lengths[:, None]
    keep = (probed[:, :, None] & live[None, :, :]).reshape(total, -1)
    table = payload.reshape(-1, pw)

    raw = jnp.einsum("sdq,sdr->qr", query_parts, decoded_parts, preferred_element_type=jnp.float32)
    values = (raw - 0.5 * sq_norm[None, :]) * score_scale
    local_peak = jnp.max(jnp.where(keep, values, floor_score), axis=1)
    weights = jnp.where(keep, jnp.exp(values - local_peak[:, None]), 0.0).astype(jnp.bfloat16)
    mass = jnp.sum(weights.astype(jnp.float32), axis=1)
    part_t = lax.dot_general(
        table, weights, (((0,), (1,)), ((), ())), preferred_element_type=jnp.float32
    )
    sendable = jnp.concatenate(
        [
            part_t.reshape(parts, chunk, total),
            jnp.broadcast_to(mass[None, None, :], (parts, 1, total)),
            jnp.broadcast_to(local_peak[None, None, :], (parts, 1, total)),
        ],
        axis=1,
    )
    pieces = lax.all_to_all(sendable, "sub", split_axis=0, concat_axis=0, tiled=True)
    peaks_in = pieces[:, chunk + 1, :]
    peak = jnp.max(peaks_in, axis=0)
    shift = jnp.exp(peaks_in - peak[None, :])
    reduced = jnp.sum(shift[:, None, :] * pieces[:, : chunk + 1, :], axis=0)
    outgoing = jnp.concatenate([reduced, peak[None, :]], axis=0)
    back = lax.all_to_all(
        outgoing.reshape(chunk + 2, groups, capacity), "cell", split_axis=1, concat_axis=1, tiled=True
    )
    back = back.reshape(chunk + 2, total)
    picked = back[:, slots]
    parts_back = picked[:chunk]
    masses = picked[chunk]
    peaks = picked[chunk + 1]
    top = jnp.max(peaks, axis=1, keepdims=True)
    scale = jnp.exp(peaks - top)
    upper = jnp.sum(scale[None, :, :] * parts_back, axis=2)
    lower = jnp.sum(scale * masses, axis=1)
    pooled = (upper / lower[None, :]).astype(jnp.bfloat16)
    return gather_by_exchange(pooled, "sub").reshape(pw, -1).T


def solution(mesh):
    placed = (
        P("cell", "sub"),
        P("cell", None),
        P("cell", None, None),
        P("cell", "sub"),
        P("sub", None, None),
        P("cell", "sub", None),
        P("cell"),
        P("cell", "sub", None),
    )
    return jax.shard_map(
        local, mesh=mesh, in_specs=placed, out_specs=P("cell", None), check_vma=False
    )
```

```python
import jax
import jax.numpy as jnp
from jax import lax
from jax.experimental import pallas as pl
from jax.sharding import PartitionSpec as P


CAP = 64


score_scale = 0.3
floor_score = -1e30


def slot_table(probe_groups, groups, capacity):
    marks = (probe_groups[:, :, None] == jnp.arange(groups, dtype=jnp.int32)[None, None, :]).astype(
        jnp.int32
    )
    routed = jnp.sum(marks, axis=1)
    earlier = jnp.cumsum(routed, axis=0) - routed
    position = jnp.sum(marks * earlier[:, None, :], axis=2)
    return probe_groups * capacity + position


def pack_slots(rows, probe_cells, slots, total):
    flat = slots.reshape(-1)
    doubled = jnp.repeat(rows, 2, axis=0)
    buffer = jnp.zeros((total, rows.shape[1]), rows.dtype).at[flat].set(doubled)
    named = probe_cells.reshape(flat.shape[0], -1).astype(jnp.bfloat16)
    cell_marks = jnp.full((total, probe_cells.shape[2]), -1.0, jnp.bfloat16).at[flat].set(named)
    return (buffer, cell_marks)


def decode_kernel(codes_ref, book_ref, base_ref, out_ref):
    m_count, width, k_count = book_ref.shape
    n = codes_ref.shape[2]
    ids = lax.broadcasted_iota(jnp.int32, (k_count, n), 0)
    for m in range(m_count):
        row = codes_ref[0, m : m + 1, :]
        onehot = (ids == row).astype(jnp.bfloat16)
        val = jnp.dot(book_ref[m], onehot, preferred_element_type=jnp.float32)
        base = base_ref[m * width : (m + 1) * width, :].astype(jnp.float32)
        out_ref[0, m * width : (m + 1) * width, :] = (val + base).astype(jnp.bfloat16)


def decode(base, codebooks, codes_blocks):
    blocks, per_block, n = codes_blocks.shape
    width, k_count = codebooks.shape[1], codebooks.shape[2]
    return pl.pallas_call(
        decode_kernel,
        grid=(blocks,),
        in_specs=[
            pl.BlockSpec((1, per_block, n), lambda p: (p, 0, 0)),
            pl.BlockSpec((per_block, width, k_count), lambda p: (p, 0, 0)),
            pl.BlockSpec((per_block * width, n), lambda p: (p, 0)),
        ],
        out_specs=pl.BlockSpec((1, per_block * width, n), lambda p: (p, 0, 0)),
        out_shape=jax.ShapeDtypeStruct((blocks, per_block * width, n), jnp.bfloat16),
    )(codes_blocks, codebooks, base)


def score_kernel(x_ref, q_ref, half_ref, keep_ref, table_ref, out_ref):
    chunk = out_ref.shape[1] - 2
    raw = lax.dot_general(
        x_ref[...], q_ref[...], (((0,), (0,)), ((), ())), preferred_element_type=jnp.float32
    )
    values = (raw - half_ref[...]) * score_scale
    keep = keep_ref[...] > 0
    peak = jnp.max(jnp.where(keep, values, floor_score), axis=0, keepdims=True)
    weights = jnp.where(keep, jnp.exp(values - peak), 0.0).astype(jnp.bfloat16)
    mass = jnp.sum(weights.astype(jnp.float32), axis=0, keepdims=True)
    part = lax.dot_general(
        table_ref[...], weights, (((0,), (0,)), ((), ())), preferred_element_type=jnp.float32
    )
    for dest in range(out_ref.shape[0]):
        out_ref[dest, :chunk, :] = part[dest * chunk : (dest + 1) * chunk, :]
        out_ref[dest, chunk : chunk + 1, :] = mass
        out_ref[dest, chunk + 1 : chunk + 2, :] = peak


def score_terms(decoded, queries_t, half_norm, keep_t, table, parts, block):
    dims, rows = decoded.shape
    total = queries_t.shape[1]
    width = table.shape[1]
    chunk = width // parts
    return pl.pallas_call(
        score_kernel,
        grid=(total // block,),
        in_specs=[
            pl.BlockSpec((dims, rows), lambda j: (0, 0)),
            pl.BlockSpec((dims, block), lambda j: (0, j)),
            pl.BlockSpec((rows, 1), lambda j: (0, 0)),
            pl.BlockSpec((rows, block), lambda j: (0, j)),
            pl.BlockSpec((rows, width), lambda j: (0, 0)),
        ],
        out_specs=pl.BlockSpec((parts, chunk + 2, block), lambda j: (0, 0, j)),
        out_shape=jax.ShapeDtypeStruct((parts, chunk + 2, total), jnp.float32),
    )(decoded, queries_t, half_norm, keep_t, table)


def gather_by_exchange(x, axis):
    count = lax.axis_size(axis)
    copies = jnp.broadcast_to(x[None], (count,) + x.shape)
    return lax.all_to_all(copies, axis, split_axis=0, concat_axis=0, tiled=True)


def local(queries, probe_groups, probe_cells, coarse, codebooks, codes, lengths, payload):
    groups = lax.axis_size("cell")
    parts = lax.axis_size("sub")
    capacity = CAP
    total = groups * capacity
    cell_dev = codes.shape[0]
    pw = payload.shape[2]
    chunk = pw // parts

    cell_count, sub_count, row_count = codes.shape
    rows_part = row_count // parts
    own_codes = codes.reshape(cell_count, sub_count, parts, rows_part)
    own_codes = jnp.transpose(own_codes, (2, 0, 1, 3)).astype(jnp.bfloat16).reshape(parts, -1)
    tables = jnp.concatenate(
        [
            own_codes,
            jnp.broadcast_to(codebooks.reshape(1, -1), (parts, codebooks.size)),
            jnp.broadcast_to(coarse.reshape(1, -1), (parts, coarse.size)),
        ],
        axis=1,
    )
    tables = lax.all_to_all(tables, "sub", split_axis=0, concat_axis=0, tiled=True)
    code_size = own_codes.shape[1]
    book_size = codebooks.size
    got_codes = tables[:, :code_size].reshape(parts, cell_count, sub_count, rows_part)
    got_codes = jnp.transpose(got_codes, (0, 2, 1, 3)).astype(jnp.int32)
    got_codes = got_codes.reshape(parts, sub_count, cell_count * rows_part)
    all_books = tables[:, code_size : code_size + book_size].reshape((-1,) + codebooks.shape[1:])
    all_coarse = tables[:, code_size + book_size :].reshape(parts, cell_count, -1)
    all_coarse = jnp.transpose(all_coarse, (1, 0, 2)).reshape(cell_count, -1)
    base = jnp.repeat(all_coarse.T, rows_part, axis=1)
    decoded_parts = decode(base, all_books, got_codes)

    slots = slot_table(probe_groups, groups, capacity)
    buffer, cell_marks = pack_slots(queries, probe_cells, slots, total)
    width = buffer.shape[1]
    arrived_all = lax.all_to_all(
        jnp.concatenate([buffer, cell_marks], axis=1).reshape(groups, -1),
        "cell",
        split_axis=0,
        concat_axis=0,
        tiled=True,
    ).reshape(total, -1)
    arrived = arrived_all[:, :width]
    arrived_cells = arrived_all[:, width:]
    query_parts = gather_by_exchange(arrived.T, "sub")
    decoded = decoded_parts.reshape(-1, decoded_parts.shape[2])
    cell_ids = arrived_cells.astype(jnp.int32)
    probed = jnp.any(
        cell_ids[:, :, None] == jnp.arange(cell_dev, dtype=jnp.int32)[None, None, :], axis=1
    )

    row_local = payload.shape[1]
    sq_norm = jnp.sum(jnp.square(decoded.astype(jnp.float32)), axis=0)
    first_row = lax.axis_index("sub") * row_local
    live = (first_row + jnp.arange(row_local, dtype=jnp.int32))[None, :] < lengths[:, None]
    keep_t = (live[:, :, None] & jnp.transpose(probed)[:, None, :]).reshape(-1, total)
    keep_t = keep_t.astype(jnp.bfloat16)
    table = payload.reshape(-1, pw)
    half_norm = (0.5 * sq_norm)[:, None]
    sendable = score_terms(
        decoded, query_parts.reshape(-1, total), half_norm, keep_t, table, parts, 256
    )
    pieces = lax.all_to_all(sendable, "sub", split_axis=0, concat_axis=0, tiled=True)
    peaks_in = pieces[:, chunk + 1, :]
    peak = jnp.max(peaks_in, axis=0)
    shift = jnp.exp(peaks_in - peak[None, :])
    reduced = jnp.sum(shift[:, None, :] * pieces[:, : chunk + 1, :], axis=0)
    outgoing = jnp.concatenate([reduced, peak[None, :]], axis=0)
    back = lax.all_to_all(
        outgoing.reshape(chunk + 2, groups, capacity), "cell", split_axis=1, concat_axis=1, tiled=True
    )
    back = back.reshape(chunk + 2, total)
    picked = back[:, slots]
    parts_back = picked[:chunk]
    masses = picked[chunk]
    peaks = picked[chunk + 1]
    top = jnp.max(peaks, axis=1, keepdims=True)
    scale = jnp.exp(peaks - top)
    upper = jnp.sum(scale[None, :, :] * parts_back, axis=2)
    lower = jnp.sum(scale * masses, axis=1)
    pooled = (upper / lower[None, :]).astype(jnp.bfloat16)
    return gather_by_exchange(pooled, "sub").reshape(pw, -1).T


def solution(mesh):
    placed = (
        P("cell", "sub"),
        P("cell", None),
        P("cell", None, None),
        P("cell", "sub"),
        P("sub", None, None),
        P("cell", "sub", None),
        P("cell"),
        P("cell", "sub", None),
    )
    return jax.shard_map(
        local, mesh=mesh, in_specs=placed, out_specs=P("cell", None), check_vma=False
    )
```

```python
import jax
import jax.numpy as jnp
from jax import lax
from jax.experimental import pallas as pl
from jax.sharding import PartitionSpec as P


CAP = 64


score_scale = 0.3
floor_score = -1e30


def slot_table(probe_groups, groups, capacity):
    marks = (probe_groups[:, :, None] == jnp.arange(groups, dtype=jnp.int32)[None, None, :]).astype(
        jnp.int32
    )
    routed = jnp.sum(marks, axis=1)
    earlier = jnp.cumsum(routed, axis=0) - routed
    position = jnp.sum(marks * earlier[:, None, :], axis=2)
    return probe_groups * capacity + position


def pack_slots(rows, probe_cells, slots, total):
    flat = slots.reshape(-1)
    doubled = jnp.repeat(rows, 2, axis=0)
    buffer = jnp.zeros((total, rows.shape[1]), rows.dtype).at[flat].set(doubled)
    named = probe_cells.reshape(flat.shape[0], -1).astype(jnp.bfloat16)
    cell_marks = jnp.full((total, probe_cells.shape[2]), -1.0, jnp.bfloat16).at[flat].set(named)
    return (buffer, cell_marks)


def decode_kernel(codes_ref, book_ref, base_ref, out_ref):
    m_count, width, k_count = book_ref.shape
    n = codes_ref.shape[2]
    ids = lax.broadcasted_iota(jnp.int32, (k_count, n), 0)
    for m in range(m_count):
        row = codes_ref[0, m : m + 1, :]
        onehot = (ids == row).astype(jnp.bfloat16)
        val = jnp.dot(book_ref[m], onehot, preferred_element_type=jnp.float32)
        base = base_ref[m * width : (m + 1) * width, :].astype(jnp.float32)
        out_ref[0, m * width : (m + 1) * width, :] = (val + base).astype(jnp.bfloat16)


def decode(base, codebooks, codes_blocks):
    blocks, per_block, n = codes_blocks.shape
    width, k_count = codebooks.shape[1], codebooks.shape[2]
    return pl.pallas_call(
        decode_kernel,
        grid=(blocks,),
        in_specs=[
            pl.BlockSpec((1, per_block, n), lambda p: (p, 0, 0)),
            pl.BlockSpec((per_block, width, k_count), lambda p: (p, 0, 0)),
            pl.BlockSpec((per_block * width, n), lambda p: (p, 0)),
        ],
        out_specs=pl.BlockSpec((1, per_block * width, n), lambda p: (p, 0, 0)),
        out_shape=jax.ShapeDtypeStruct((blocks, per_block * width, n), jnp.bfloat16),
    )(codes_blocks, codebooks, base)


def score_kernel(x_ref, q_ref, half_ref, keep_ref, table_ref, out_ref):
    chunk = out_ref.shape[1] - 2
    raw = jnp.dot(x_ref[...], q_ref[...], preferred_element_type=jnp.float32)
    values = (raw - half_ref[...]) * score_scale
    keep = keep_ref[...] > 0
    peak = jnp.max(jnp.where(keep, values, floor_score), axis=0, keepdims=True)
    weights = jnp.where(keep, jnp.exp(values - peak), 0.0).astype(jnp.bfloat16)
    mass = jnp.sum(weights.astype(jnp.float32), axis=0, keepdims=True)
    part = jnp.dot(table_ref[...], weights, preferred_element_type=jnp.float32)
    for dest in range(out_ref.shape[0]):
        out_ref[dest, :chunk, :] = part[dest * chunk : (dest + 1) * chunk, :]
        out_ref[dest, chunk : chunk + 1, :] = mass
        out_ref[dest, chunk + 1 : chunk + 2, :] = peak


def score_terms(decoded_t, queries_t, half_norm, keep_t, table_t, parts, block):
    rows, dims = decoded_t.shape
    total = queries_t.shape[1]
    width = table_t.shape[0]
    chunk = width // parts
    return pl.pallas_call(
        score_kernel,
        grid=(total // block,),
        in_specs=[
            pl.BlockSpec((rows, dims), lambda j: (0, 0)),
            pl.BlockSpec((dims, block), lambda j: (0, j)),
            pl.BlockSpec((rows, 1), lambda j: (0, 0)),
            pl.BlockSpec((rows, block), lambda j: (0, j)),
            pl.BlockSpec((width, rows), lambda j: (0, 0)),
        ],
        out_specs=pl.BlockSpec((parts, chunk + 2, block), lambda j: (0, 0, j)),
        out_shape=jax.ShapeDtypeStruct((parts, chunk + 2, total), jnp.float32),
    )(decoded_t, queries_t, half_norm, keep_t, table_t)


def gather_by_exchange(x, axis):
    count = lax.axis_size(axis)
    copies = jnp.broadcast_to(x[None], (count,) + x.shape)
    return lax.all_to_all(copies, axis, split_axis=0, concat_axis=0, tiled=True)


def local(queries, probe_groups, probe_cells, coarse, codebooks, codes, lengths, payload):
    groups = lax.axis_size("cell")
    parts = lax.axis_size("sub")
    capacity = CAP
    total = groups * capacity
    cell_dev = codes.shape[0]
    pw = payload.shape[2]
    chunk = pw // parts

    cell_count, sub_count, row_count = codes.shape
    rows_part = row_count // parts
    own_codes = codes.reshape(cell_count, sub_count, parts, rows_part)
    own_codes = jnp.transpose(own_codes, (2, 0, 1, 3)).astype(jnp.bfloat16).reshape(parts, -1)
    tables = jnp.concatenate(
        [
            own_codes,
            jnp.broadcast_to(codebooks.reshape(1, -1), (parts, codebooks.size)),
            jnp.broadcast_to(coarse.reshape(1, -1), (parts, coarse.size)),
        ],
        axis=1,
    )
    tables = lax.all_to_all(tables, "sub", split_axis=0, concat_axis=0, tiled=True)
    code_size = own_codes.shape[1]
    book_size = codebooks.size
    got_codes = tables[:, :code_size].reshape(parts, cell_count, sub_count, rows_part)
    got_codes = jnp.transpose(got_codes, (0, 2, 1, 3)).astype(jnp.int32)
    got_codes = got_codes.reshape(parts, sub_count, cell_count * rows_part)
    all_books = tables[:, code_size : code_size + book_size].reshape((-1,) + codebooks.shape[1:])
    all_coarse = tables[:, code_size + book_size :].reshape(parts, cell_count, -1)
    all_coarse = jnp.transpose(all_coarse, (1, 0, 2)).reshape(cell_count, -1)
    base = jnp.repeat(all_coarse.T, rows_part, axis=1)
    decoded_parts = decode(base, all_books, got_codes)

    slots = slot_table(probe_groups, groups, capacity)
    buffer, cell_marks = pack_slots(queries, probe_cells, slots, total)
    width = buffer.shape[1]
    arrived_all = lax.all_to_all(
        jnp.concatenate([buffer, cell_marks], axis=1).reshape(groups, -1),
        "cell",
        split_axis=0,
        concat_axis=0,
        tiled=True,
    ).reshape(total, -1)
    arrived = arrived_all[:, :width]
    arrived_cells = arrived_all[:, width:]
    query_parts = gather_by_exchange(arrived.T, "sub")
    decoded = decoded_parts.reshape(-1, decoded_parts.shape[2])
    cell_ids = arrived_cells.astype(jnp.int32)
    probed = jnp.any(
        cell_ids[:, :, None] == jnp.arange(cell_dev, dtype=jnp.int32)[None, None, :], axis=1
    )

    row_local = payload.shape[1]
    sq_norm = jnp.sum(jnp.square(decoded.astype(jnp.float32)), axis=0)
    first_row = lax.axis_index("sub") * row_local
    live = (first_row + jnp.arange(row_local, dtype=jnp.int32))[None, :] < lengths[:, None]
    keep_t = (live[:, :, None] & jnp.transpose(probed)[:, None, :]).reshape(-1, total)
    keep_t = keep_t.astype(jnp.bfloat16)
    table = payload.reshape(-1, pw)
    half_norm = (0.5 * sq_norm)[:, None]
    sendable = score_terms(
        decoded.T, query_parts.reshape(-1, total), half_norm, keep_t, table.T, parts, 512
    )
    pieces = lax.all_to_all(sendable, "sub", split_axis=0, concat_axis=0, tiled=True)
    peaks_in = pieces[:, chunk + 1, :]
    peak = jnp.max(peaks_in, axis=0)
    shift = jnp.exp(peaks_in - peak[None, :])
    reduced = jnp.sum(shift[:, None, :] * pieces[:, : chunk + 1, :], axis=0)
    outgoing = jnp.concatenate([reduced, peak[None, :]], axis=0)
    back = lax.all_to_all(
        outgoing.reshape(chunk + 2, groups, capacity), "cell", split_axis=1, concat_axis=1, tiled=True
    )
    back = back.reshape(chunk + 2, total)
    picked = back[:, slots]
    parts_back = picked[:chunk]
    masses = picked[chunk]
    peaks = picked[chunk + 1]
    top = jnp.max(peaks, axis=1, keepdims=True)
    scale = jnp.exp(peaks - top)
    upper = jnp.sum(scale[None, :, :] * parts_back, axis=2)
    lower = jnp.sum(scale * masses, axis=1)
    pooled = (upper / lower[None, :]).astype(jnp.bfloat16)
    return gather_by_exchange(pooled, "sub").reshape(pw, -1).T


def solution(mesh):
    placed = (
        P("cell", "sub"),
        P("cell", None),
        P("cell", None, None),
        P("cell", "sub"),
        P("sub", None, None),
        P("cell", "sub", None),
        P("cell"),
        P("cell", "sub", None),
    )
    return jax.shard_map(
        local, mesh=mesh, in_specs=placed, out_specs=P("cell", None), check_vma=False
    )
```

```python
import jax
import jax.numpy as jnp
from jax import lax
from jax.experimental import pallas as pl
from jax.sharding import PartitionSpec as P


CAP = 64


score_scale = 0.3
floor_score = -1e30


def slot_table(probe_groups, groups, capacity):
    marks = (probe_groups[:, :, None] == jnp.arange(groups, dtype=jnp.int32)[None, None, :]).astype(
        jnp.int32
    )
    routed = jnp.sum(marks, axis=1)
    earlier = jnp.cumsum(routed, axis=0) - routed
    position = jnp.sum(marks * earlier[:, None, :], axis=2)
    return probe_groups * capacity + position


def pack_slots(rows, probe_cells, slots, total):
    flat = slots.reshape(-1)
    doubled = jnp.repeat(rows, 2, axis=0)
    buffer = jnp.zeros((total, rows.shape[1]), rows.dtype).at[flat].set(doubled)
    named = probe_cells.reshape(flat.shape[0], -1).astype(jnp.bfloat16)
    cell_marks = jnp.full((total, probe_cells.shape[2]), -1.0, jnp.bfloat16).at[flat].set(named)
    return (buffer, cell_marks)


def decode_kernel(codes_ref, book_ref, base_ref, out_ref):
    m_count, width, k_count = book_ref.shape
    n = codes_ref.shape[2]
    ids = lax.broadcasted_iota(jnp.int32, (k_count, n), 0)
    for m in range(m_count):
        row = codes_ref[0, m : m + 1, :]
        onehot = (ids == row).astype(jnp.bfloat16)
        val = jnp.dot(book_ref[m], onehot, preferred_element_type=jnp.float32)
        base = base_ref[m * width : (m + 1) * width, :].astype(jnp.float32)
        out_ref[0, m * width : (m + 1) * width, :] = (val + base).astype(jnp.bfloat16)


def decode(base, codebooks, codes_blocks):
    blocks, per_block, n = codes_blocks.shape
    width, k_count = codebooks.shape[1], codebooks.shape[2]
    return pl.pallas_call(
        decode_kernel,
        grid=(blocks,),
        in_specs=[
            pl.BlockSpec((1, per_block, n), lambda p: (p, 0, 0)),
            pl.BlockSpec((per_block, width, k_count), lambda p: (p, 0, 0)),
            pl.BlockSpec((per_block * width, n), lambda p: (p, 0)),
        ],
        out_specs=pl.BlockSpec((1, per_block * width, n), lambda p: (p, 0, 0)),
        out_shape=jax.ShapeDtypeStruct((blocks, per_block * width, n), jnp.bfloat16),
    )(codes_blocks, codebooks, base)


def score_kernel(x_ref, q_ref, half_ref, keep_ref, table_ref, out_ref):
    chunk = out_ref.shape[1] - 2
    raw = jnp.dot(x_ref[...], q_ref[...], preferred_element_type=jnp.float32)
    values = (raw - half_ref[...]) * score_scale
    keep = keep_ref[...] > 0
    peak = jnp.max(jnp.where(keep, values, floor_score), axis=0, keepdims=True)
    weights = jnp.where(keep, jnp.exp(values - peak), 0.0).astype(jnp.bfloat16)
    mass = jnp.sum(weights.astype(jnp.float32), axis=0, keepdims=True)
    part = jnp.dot(table_ref[...], weights, preferred_element_type=jnp.float32)
    for dest in range(out_ref.shape[0]):
        out_ref[dest, :chunk, :] = part[dest * chunk : (dest + 1) * chunk, :]
        out_ref[dest, chunk : chunk + 1, :] = mass
        out_ref[dest, chunk + 1 : chunk + 2, :] = peak


def score_terms(decoded_t, queries_t, half_norm, keep_t, table_t, parts, block):
    rows, dims = decoded_t.shape
    total = queries_t.shape[1]
    width = table_t.shape[0]
    chunk = width // parts
    return pl.pallas_call(
        score_kernel,
        grid=(total // block,),
        in_specs=[
            pl.BlockSpec((rows, dims), lambda j: (0, 0)),
            pl.BlockSpec((dims, block), lambda j: (0, j)),
            pl.BlockSpec((rows, 1), lambda j: (0, 0)),
            pl.BlockSpec((rows, block), lambda j: (0, j)),
            pl.BlockSpec((width, rows), lambda j: (0, 0)),
        ],
        out_specs=pl.BlockSpec((parts, chunk + 2, block), lambda j: (0, 0, j)),
        out_shape=jax.ShapeDtypeStruct((parts, chunk + 2, total), jnp.float32),
    )(decoded_t, queries_t, half_norm, keep_t, table_t)


def gather_by_exchange(x, axis):
    count = lax.axis_size(axis)
    copies = jnp.broadcast_to(x[None], (count,) + x.shape)
    return lax.all_to_all(copies, axis, split_axis=0, concat_axis=0, tiled=True)


def local(queries, probe_groups, probe_cells, coarse, codebooks, codes, lengths, payload):
    groups = lax.axis_size("cell")
    parts = lax.axis_size("sub")
    capacity = CAP
    total = groups * capacity
    cell_dev = codes.shape[0]
    pw = payload.shape[2]
    chunk = pw // parts

    cell_count, sub_count, row_count = codes.shape
    rows_part = row_count // parts
    own_codes = codes.reshape(cell_count, sub_count, parts, rows_part)
    own_codes = jnp.transpose(own_codes, (2, 0, 1, 3)).astype(jnp.bfloat16).reshape(parts, -1, 128)
    tables = jnp.concatenate(
        [
            own_codes,
            jnp.broadcast_to(codebooks.reshape(1, -1, 128), (parts, codebooks.size // 128, 128)),
            jnp.broadcast_to(coarse.reshape(1, -1, 128), (parts, coarse.size // 128, 128)),
        ],
        axis=1,
    )
    tables = lax.all_to_all(tables, "sub", split_axis=0, concat_axis=0, tiled=True)
    tables = tables.reshape(parts, -1)
    code_size = own_codes.shape[1] * own_codes.shape[2]
    book_size = codebooks.size
    got_codes = tables[:, :code_size].reshape(parts, cell_count, sub_count, rows_part)
    got_codes = jnp.transpose(got_codes, (0, 2, 1, 3)).astype(jnp.int32)
    got_codes = got_codes.reshape(parts, sub_count, cell_count * rows_part)
    all_books = tables[:, code_size : code_size + book_size].reshape((-1,) + codebooks.shape[1:])
    all_coarse = tables[:, code_size + book_size :].reshape(parts, cell_count, -1)
    all_coarse = jnp.transpose(all_coarse, (1, 0, 2)).reshape(cell_count, -1)
    base = jnp.repeat(all_coarse.T, rows_part, axis=1)
    decoded_parts = decode(base, all_books, got_codes)

    slots = slot_table(probe_groups, groups, capacity)
    buffer, cell_marks = pack_slots(queries, probe_cells, slots, total)
    width = buffer.shape[1]
    arrived_all = lax.all_to_all(
        jnp.concatenate([buffer, cell_marks], axis=1).reshape(groups, -1),
        "cell",
        split_axis=0,
        concat_axis=0,
        tiled=True,
    ).reshape(total, -1)
    arrived = arrived_all[:, :width]
    arrived_cells = arrived_all[:, width:]
    query_parts = gather_by_exchange(arrived.T, "sub")
    decoded = decoded_parts.reshape(-1, decoded_parts.shape[2])
    cell_ids = arrived_cells.astype(jnp.int32)
    probed = jnp.any(
        cell_ids[:, :, None] == jnp.arange(cell_dev, dtype=jnp.int32)[None, None, :], axis=1
    )

    row_local = payload.shape[1]
    sq_norm = jnp.sum(jnp.square(decoded.astype(jnp.float32)), axis=0)
    first_row = lax.axis_index("sub") * row_local
    live = (first_row + jnp.arange(row_local, dtype=jnp.int32))[None, :] < lengths[:, None]
    keep_t = (live[:, :, None] & jnp.transpose(probed)[:, None, :]).reshape(-1, total)
    keep_t = keep_t.astype(jnp.bfloat16)
    table = payload.reshape(-1, pw)
    half_norm = (0.5 * sq_norm)[:, None]
    sendable = score_terms(
        decoded.T, query_parts.reshape(-1, total), half_norm, keep_t, table.T, parts, 512
    )
    pieces = lax.all_to_all(sendable, "sub", split_axis=0, concat_axis=0, tiled=True)
    peaks_in = pieces[:, chunk + 1, :]
    peak = jnp.max(peaks_in, axis=0)
    shift = jnp.exp(peaks_in - peak[None, :])
    reduced = jnp.sum(shift[:, None, :] * pieces[:, : chunk + 1, :], axis=0)
    outgoing = jnp.concatenate([reduced, peak[None, :]], axis=0)
    back = lax.all_to_all(
        outgoing.reshape(chunk + 2, groups, capacity), "cell", split_axis=1, concat_axis=1, tiled=True
    )
    back = back.reshape(chunk + 2, total)
    picked = back[:, slots]
    parts_back = picked[:chunk]
    masses = picked[chunk]
    peaks = picked[chunk + 1]
    top = jnp.max(peaks, axis=1, keepdims=True)
    scale = jnp.exp(peaks - top)
    upper = jnp.sum(scale[None, :, :] * parts_back, axis=2)
    lower = jnp.sum(scale * masses, axis=1)
    pooled = (upper / lower[None, :]).T.astype(jnp.bfloat16)
    copies = jnp.broadcast_to(pooled[None], (parts,) + pooled.shape)
    gathered = lax.all_to_all(copies, "sub", split_axis=0, concat_axis=2, tiled=True)
    return gathered.reshape(pooled.shape[0], pw)


def solution(mesh):
    placed = (
        P("cell", "sub"),
        P("cell", None),
        P("cell", None, None),
        P("cell", "sub"),
        P("sub", None, None),
        P("cell", "sub", None),
        P("cell"),
        P("cell", "sub", None),
    )
    return jax.shard_map(
        local, mesh=mesh, in_specs=placed, out_specs=P("cell", None), check_vma=False
    )
```

```python
import jax
import jax.numpy as jnp
from jax import lax
from jax.experimental import pallas as pl
from jax.sharding import PartitionSpec as P


CAP = 64


score_scale = 0.3
floor_score = -1e30


def slot_table(probe_groups, groups, capacity):
    marks = (probe_groups[:, :, None] == jnp.arange(groups, dtype=jnp.int32)[None, None, :]).astype(
        jnp.int32
    )
    routed = jnp.sum(marks, axis=1)
    earlier = jnp.cumsum(routed, axis=0) - routed
    position = jnp.sum(marks * earlier[:, None, :], axis=2)
    return probe_groups * capacity + position


def pack_slots(rows, probe_cells, slots, total):
    flat = slots.reshape(-1)
    doubled = jnp.repeat(rows, 2, axis=0)
    buffer = jnp.zeros((total, rows.shape[1]), rows.dtype).at[flat].set(doubled)
    named = probe_cells.reshape(flat.shape[0], -1).astype(jnp.bfloat16)
    cell_marks = jnp.full((total, probe_cells.shape[2]), -1.0, jnp.bfloat16).at[flat].set(named)
    return (buffer, cell_marks)


def decode_kernel(codes_ref, book_ref, base_ref, out_ref):
    m_count, width, k_count = book_ref.shape
    n = codes_ref.shape[2]
    ids = lax.broadcasted_iota(jnp.int32, (k_count, n), 0)
    for m in range(m_count):
        row = codes_ref[0, m : m + 1, :]
        onehot = (ids == row).astype(jnp.bfloat16)
        val = jnp.dot(book_ref[m], onehot, preferred_element_type=jnp.float32)
        base = base_ref[m * width : (m + 1) * width, :].astype(jnp.float32)
        out_ref[0, m * width : (m + 1) * width, :] = (val + base).astype(jnp.bfloat16)


def decode(base, codebooks, codes_blocks):
    blocks, per_block, n = codes_blocks.shape
    width, k_count = codebooks.shape[1], codebooks.shape[2]
    return pl.pallas_call(
        decode_kernel,
        grid=(blocks,),
        in_specs=[
            pl.BlockSpec((1, per_block, n), lambda p: (p, 0, 0)),
            pl.BlockSpec((per_block, width, k_count), lambda p: (p, 0, 0)),
            pl.BlockSpec((per_block * width, n), lambda p: (p, 0)),
        ],
        out_specs=pl.BlockSpec((1, per_block * width, n), lambda p: (p, 0, 0)),
        out_shape=jax.ShapeDtypeStruct((blocks, per_block * width, n), jnp.bfloat16),
    )(codes_blocks, codebooks, base)


def score_kernel(x_ref, q_ref, half_ref, keep_ref, table_ref, out_ref):
    chunk = out_ref.shape[1] - 2
    raw = jnp.dot(x_ref[...], q_ref[...], preferred_element_type=jnp.float32)
    values = (raw - half_ref[...]) * score_scale
    keep = keep_ref[...] > 0
    peak = jnp.max(jnp.where(keep, values, floor_score), axis=0, keepdims=True)
    weights = jnp.where(keep, jnp.exp(values - peak), 0.0).astype(jnp.bfloat16)
    part = jnp.dot(table_ref[...], weights, preferred_element_type=jnp.float32)
    width = out_ref.shape[0] * chunk
    mass = part[width : width + 1, :]
    for dest in range(out_ref.shape[0]):
        out_ref[dest, :chunk, :] = part[dest * chunk : (dest + 1) * chunk, :]
        out_ref[dest, chunk : chunk + 1, :] = mass
        out_ref[dest, chunk + 1 : chunk + 2, :] = peak


def score_terms(decoded_t, queries_t, half_norm, keep_t, table_t, parts, block):
    rows, dims = decoded_t.shape
    total = queries_t.shape[1]
    width = table_t.shape[0]
    chunk = width // parts
    extra = jnp.zeros((16, rows), table_t.dtype).at[0].set(1)
    table_t = jnp.concatenate([table_t, extra], axis=0)
    return pl.pallas_call(
        score_kernel,
        grid=(total // block,),
        in_specs=[
            pl.BlockSpec((rows, dims), lambda j: (0, 0)),
            pl.BlockSpec((dims, block), lambda j: (0, j)),
            pl.BlockSpec((rows, 1), lambda j: (0, 0)),
            pl.BlockSpec((rows, block), lambda j: (0, j)),
            pl.BlockSpec((width + 16, rows), lambda j: (0, 0)),
        ],
        out_specs=pl.BlockSpec((parts, chunk + 2, block), lambda j: (0, 0, j)),
        out_shape=jax.ShapeDtypeStruct((parts, chunk + 2, total), jnp.float32),
    )(decoded_t, queries_t, half_norm, keep_t, table_t)


def gather_by_exchange(x, axis):
    count = lax.axis_size(axis)
    copies = jnp.broadcast_to(x[None], (count,) + x.shape)
    return lax.all_to_all(copies, axis, split_axis=0, concat_axis=0, tiled=True)


def local(queries, probe_groups, probe_cells, coarse, codebooks, codes, lengths, payload):
    groups = lax.axis_size("cell")
    parts = lax.axis_size("sub")
    capacity = CAP
    total = groups * capacity
    cell_dev = codes.shape[0]
    pw = payload.shape[2]
    chunk = pw // parts

    cell_count, sub_count, row_count = codes.shape
    rows_part = row_count // parts
    own_codes = codes.reshape(cell_count, sub_count, parts, rows_part)
    own_codes = jnp.transpose(own_codes, (2, 0, 1, 3)).astype(jnp.bfloat16).reshape(parts, -1, 128)
    tables = jnp.concatenate(
        [
            own_codes,
            jnp.broadcast_to(codebooks.reshape(1, -1, 128), (parts, codebooks.size // 128, 128)),
            jnp.broadcast_to(coarse.reshape(1, -1, 128), (parts, coarse.size // 128, 128)),
        ],
        axis=1,
    )
    tables = lax.all_to_all(tables, "sub", split_axis=0, concat_axis=0, tiled=True)
    tables = tables.reshape(parts, -1)
    code_size = own_codes.shape[1] * own_codes.shape[2]
    book_size = codebooks.size
    got_codes = tables[:, :code_size].reshape(parts, cell_count, sub_count, rows_part)
    got_codes = jnp.transpose(got_codes, (0, 2, 1, 3)).astype(jnp.int32)
    got_codes = got_codes.reshape(parts, sub_count, cell_count * rows_part)
    all_books = tables[:, code_size : code_size + book_size].reshape((-1,) + codebooks.shape[1:])
    all_coarse = tables[:, code_size + book_size :].reshape(parts, cell_count, -1)
    all_coarse = jnp.transpose(all_coarse, (1, 0, 2)).reshape(cell_count, -1)
    base = jnp.repeat(all_coarse.T, rows_part, axis=1)
    decoded_parts = decode(base, all_books, got_codes)

    slots = slot_table(probe_groups, groups, capacity)
    buffer, cell_marks = pack_slots(queries, probe_cells, slots, total)
    width = buffer.shape[1]
    arrived_all = lax.all_to_all(
        jnp.concatenate([buffer, cell_marks], axis=1).reshape(groups, -1),
        "cell",
        split_axis=0,
        concat_axis=0,
        tiled=True,
    ).reshape(total, -1)
    arrived = arrived_all[:, :width]
    arrived_cells = arrived_all[:, width:]
    query_parts = gather_by_exchange(arrived.T, "sub")
    decoded = decoded_parts.reshape(-1, decoded_parts.shape[2])
    cell_ids = arrived_cells.astype(jnp.int32)
    probed = jnp.any(
        cell_ids[:, :, None] == jnp.arange(cell_dev, dtype=jnp.int32)[None, None, :], axis=1
    )

    row_local = payload.shape[1]
    sq_norm = jnp.sum(jnp.square(decoded.astype(jnp.float32)), axis=0)
    first_row = lax.axis_index("sub") * row_local
    live = (first_row + jnp.arange(row_local, dtype=jnp.int32))[None, :] < lengths[:, None]
    keep_t = (live[:, :, None] & jnp.transpose(probed)[:, None, :]).reshape(-1, total)
    keep_t = keep_t.astype(jnp.bfloat16)
    table = payload.reshape(-1, pw)
    half_norm = (0.5 * sq_norm)[:, None]
    sendable = score_terms(
        decoded.T, query_parts.reshape(-1, total), half_norm, keep_t, table.T, parts, 256
    )
    pieces = lax.all_to_all(sendable, "sub", split_axis=0, concat_axis=0, tiled=True)
    peaks_in = pieces[:, chunk + 1, :]
    peak = jnp.max(peaks_in, axis=0)
    shift = jnp.exp(peaks_in - peak[None, :])
    reduced = jnp.sum(shift[:, None, :] * pieces[:, : chunk + 1, :], axis=0)
    outgoing = jnp.concatenate([reduced, peak[None, :]], axis=0)
    back = lax.all_to_all(
        outgoing.reshape(chunk + 2, groups, capacity), "cell", split_axis=1, concat_axis=1, tiled=True
    )
    back = back.reshape(chunk + 2, total)
    picked = back[:, slots]
    parts_back = picked[:chunk]
    masses = picked[chunk]
    peaks = picked[chunk + 1]
    top = jnp.max(peaks, axis=1, keepdims=True)
    scale = jnp.exp(peaks - top)
    upper = jnp.sum(scale[None, :, :] * parts_back, axis=2)
    lower = jnp.sum(scale * masses, axis=1)
    pooled = (upper / lower[None, :]).T.astype(jnp.bfloat16)
    copies = jnp.broadcast_to(pooled[None], (parts,) + pooled.shape)
    gathered = lax.all_to_all(copies, "sub", split_axis=0, concat_axis=2, tiled=True)
    return gathered.reshape(pooled.shape[0], pw)


def solution(mesh):
    placed = (
        P("cell", "sub"),
        P("cell", None),
        P("cell", None, None),
        P("cell", "sub"),
        P("sub", None, None),
        P("cell", "sub", None),
        P("cell"),
        P("cell", "sub", None),
    )
    return jax.shard_map(
        local, mesh=mesh, in_specs=placed, out_specs=P("cell", None), check_vma=False
    )
```

```python
import jax
import jax.numpy as jnp
from jax import lax
from jax.experimental import pallas as pl
from jax.sharding import PartitionSpec as P


CAP = 64


score_scale = 0.3
floor_score = -1e30


def slot_table(probe_groups, groups, capacity):
    marks = (probe_groups[:, :, None] == jnp.arange(groups, dtype=jnp.int32)[None, None, :]).astype(
        jnp.int32
    )
    routed = jnp.sum(marks, axis=1)
    earlier = jnp.cumsum(routed, axis=0) - routed
    position = jnp.sum(marks * earlier[:, None, :], axis=2)
    return probe_groups * capacity + position


def pack_slots(rows, probe_cells, slots, total):
    flat = slots.reshape(-1)
    doubled = jnp.repeat(rows, 2, axis=0)
    buffer = jnp.zeros((total, rows.shape[1]), rows.dtype).at[flat].set(doubled)
    named = probe_cells.reshape(flat.shape[0], -1).astype(jnp.bfloat16)
    cell_marks = jnp.full((total, probe_cells.shape[2]), -1.0, jnp.bfloat16).at[flat].set(named)
    return (buffer, cell_marks)


def decode_kernel(codes_ref, book_ref, base_ref, out_ref):
    m_count, width, k_count = book_ref.shape
    n = codes_ref.shape[2]
    ids = lax.broadcasted_iota(jnp.int32, (k_count, n), 0)
    for m in range(m_count):
        row = codes_ref[0, m : m + 1, :]
        onehot = (ids == row).astype(jnp.bfloat16)
        val = jnp.dot(book_ref[m], onehot, preferred_element_type=jnp.float32)
        base = base_ref[m * width : (m + 1) * width, :].astype(jnp.float32)
        out_ref[0, m * width : (m + 1) * width, :] = (val + base).astype(jnp.bfloat16)


def decode(base, codebooks, codes_blocks):
    blocks, per_block, n = codes_blocks.shape
    width, k_count = codebooks.shape[1], codebooks.shape[2]
    return pl.pallas_call(
        decode_kernel,
        grid=(blocks,),
        in_specs=[
            pl.BlockSpec((1, per_block, n), lambda p: (p, 0, 0)),
            pl.BlockSpec((per_block, width, k_count), lambda p: (p, 0, 0)),
            pl.BlockSpec((per_block * width, n), lambda p: (p, 0)),
        ],
        out_specs=pl.BlockSpec((1, per_block * width, n), lambda p: (p, 0, 0)),
        out_shape=jax.ShapeDtypeStruct((blocks, per_block * width, n), jnp.bfloat16),
    )(codes_blocks, codebooks, base)


def gather_by_exchange(x, axis):
    count = lax.axis_size(axis)
    copies = jnp.broadcast_to(x[None], (count,) + x.shape)
    return lax.all_to_all(copies, axis, split_axis=0, concat_axis=0, tiled=True)


def local(queries, probe_groups, probe_cells, coarse, codebooks, codes, lengths, payload):
    groups = lax.axis_size("cell")
    parts = lax.axis_size("sub")
    capacity = CAP
    total = groups * capacity
    cell_dev = codes.shape[0]
    pw = payload.shape[2]
    chunk = pw // parts

    cell_count, sub_count, row_count = codes.shape
    rows_part = row_count // parts
    own_codes = codes.reshape(cell_count, sub_count, parts, rows_part)
    own_codes = jnp.transpose(own_codes, (2, 0, 1, 3)).astype(jnp.bfloat16).reshape(parts, -1, 128)
    tables = jnp.concatenate(
        [
            own_codes,
            jnp.broadcast_to(codebooks.reshape(1, -1, 128), (parts, codebooks.size // 128, 128)),
            jnp.broadcast_to(coarse.reshape(1, -1, 128), (parts, coarse.size // 128, 128)),
        ],
        axis=1,
    )
    tables = lax.all_to_all(tables, "sub", split_axis=0, concat_axis=0, tiled=True)
    tables = tables.reshape(parts, -1)
    code_size = own_codes.shape[1] * own_codes.shape[2]
    book_size = codebooks.size
    got_codes = tables[:, :code_size].reshape(parts, cell_count, sub_count, rows_part)
    got_codes = jnp.transpose(got_codes, (0, 2, 1, 3)).astype(jnp.int32)
    got_codes = got_codes.reshape(parts, sub_count, cell_count * rows_part)
    all_books = tables[:, code_size : code_size + book_size].reshape((-1,) + codebooks.shape[1:])
    all_coarse = tables[:, code_size + book_size :].reshape(parts, cell_count, -1)
    all_coarse = jnp.transpose(all_coarse, (1, 0, 2)).reshape(cell_count, -1)
    base = jnp.repeat(all_coarse.T, rows_part, axis=1)
    decoded_parts = decode(base, all_books, got_codes)

    slots = slot_table(probe_groups, groups, capacity)
    buffer, cell_marks = pack_slots(queries, probe_cells, slots, total)
    width = buffer.shape[1]
    arrived_all = lax.all_to_all(
        jnp.concatenate([buffer, cell_marks], axis=1).reshape(groups, -1),
        "cell",
        split_axis=0,
        concat_axis=0,
        tiled=True,
    ).reshape(total, -1)
    arrived = arrived_all[:, :width]
    arrived_cells = arrived_all[:, width:]
    query_parts = gather_by_exchange(arrived.T, "sub")
    decoded = decoded_parts.reshape(-1, decoded_parts.shape[2])
    cell_ids = arrived_cells.astype(jnp.int32)
    probed = jnp.any(
        cell_ids[:, :, None] == jnp.arange(cell_dev, dtype=jnp.int32)[None, None, :], axis=1
    )

    row_local = payload.shape[1]
    sq_norm = jnp.sum(jnp.square(decoded.astype(jnp.float32)), axis=0)
    first_row = lax.axis_index("sub") * row_local
    live = (first_row + jnp.arange(row_local, dtype=jnp.int32))[None, :] < lengths[:, None]
    keep = (probed[:, :, None] & live[None, :, :]).reshape(total, -1)
    table = payload.reshape(-1, pw)

    raw = jnp.einsum("sdq,sdr->qr", query_parts, decoded_parts, preferred_element_type=jnp.float32)
    values = (raw - 0.5 * sq_norm[None, :]) * score_scale
    local_peak = jnp.max(jnp.where(keep, values, floor_score), axis=1)
    weights = jnp.where(keep, jnp.exp(values - local_peak[:, None]), 0.0).astype(jnp.bfloat16)
    mass = jnp.sum(weights.astype(jnp.float32), axis=1)
    part_t = lax.dot_general(
        table, weights, (((0,), (1,)), ((), ())), preferred_element_type=jnp.float32
    )
    sendable = jnp.concatenate(
        [
            part_t.reshape(parts, chunk, total),
            jnp.broadcast_to(mass[None, None, :], (parts, 1, total)),
            jnp.broadcast_to(local_peak[None, None, :], (parts, 1, total)),
        ],
        axis=1,
    )
    pieces = lax.all_to_all(
        sendable.reshape(parts, -1, 128), "sub", split_axis=0, concat_axis=0, tiled=True
    ).reshape(sendable.shape)
    peaks_in = pieces[:, chunk + 1, :]
    peak = jnp.max(peaks_in, axis=0)
    shift = jnp.exp(peaks_in - peak[None, :])
    reduced = jnp.sum(shift[:, None, :] * pieces[:, : chunk + 1, :], axis=0)
    outgoing = jnp.concatenate([reduced, peak[None, :]], axis=0)
    back = lax.all_to_all(
        outgoing.reshape(chunk + 2, groups, capacity), "cell", split_axis=1, concat_axis=1, tiled=True
    )
    back = back.reshape(chunk + 2, total)
    picked = back[:, slots]
    parts_back = picked[:chunk]
    masses = picked[chunk]
    peaks = picked[chunk + 1]
    top = jnp.max(peaks, axis=1, keepdims=True)
    scale = jnp.exp(peaks - top)
    upper = jnp.sum(scale[None, :, :] * parts_back, axis=2)
    lower = jnp.sum(scale * masses, axis=1)
    pooled = (upper / lower[None, :]).T.astype(jnp.bfloat16)
    copies = jnp.broadcast_to(pooled[None], (parts,) + pooled.shape)
    gathered = lax.all_to_all(copies, "sub", split_axis=0, concat_axis=2, tiled=True)
    return gathered.reshape(pooled.shape[0], pw)


def solution(mesh):
    placed = (
        P("cell", "sub"),
        P("cell", None),
        P("cell", None, None),
        P("cell", "sub"),
        P("sub", None, None),
        P("cell", "sub", None),
        P("cell"),
        P("cell", "sub", None),
    )
    return jax.shard_map(
        local, mesh=mesh, in_specs=placed, out_specs=P("cell", None), check_vma=False
    )
```

```python
import jax
import jax.numpy as jnp
from jax import lax
from jax.experimental import pallas as pl
from jax.sharding import PartitionSpec as P


CAP = 64


score_scale = 0.3
floor_score = -1e30


def slot_table(probe_groups, groups, capacity):
    marks = (probe_groups[:, :, None] == jnp.arange(groups, dtype=jnp.int32)[None, None, :]).astype(
        jnp.int32
    )
    routed = jnp.sum(marks, axis=1)
    earlier = jnp.cumsum(routed, axis=0) - routed
    position = jnp.sum(marks * earlier[:, None, :], axis=2)
    return probe_groups * capacity + position


def pack_slots(rows, probe_cells, slots, total):
    flat = slots.reshape(-1)
    doubled = jnp.repeat(rows, 2, axis=0)
    buffer = jnp.zeros((total, rows.shape[1]), rows.dtype).at[flat].set(doubled)
    named = probe_cells.reshape(flat.shape[0], -1).astype(jnp.bfloat16)
    cell_marks = jnp.full((total, probe_cells.shape[2]), -1.0, jnp.bfloat16).at[flat].set(named)
    return (buffer, cell_marks)


def decode_kernel(codes_ref, book_ref, base_ref, out_ref):
    m_count, width, k_count = book_ref.shape
    n = codes_ref.shape[2]
    ids = lax.broadcasted_iota(jnp.int32, (k_count, n), 0)
    for m in range(m_count):
        row = codes_ref[0, m : m + 1, :]
        onehot = (ids == row).astype(jnp.bfloat16)
        val = jnp.dot(book_ref[m], onehot, preferred_element_type=jnp.float32)
        base = base_ref[m * width : (m + 1) * width, :].astype(jnp.float32)
        out_ref[0, m * width : (m + 1) * width, :] = (val + base).astype(jnp.bfloat16)


def decode(base, codebooks, codes_blocks):
    blocks, per_block, n = codes_blocks.shape
    width, k_count = codebooks.shape[1], codebooks.shape[2]
    return pl.pallas_call(
        decode_kernel,
        grid=(blocks,),
        in_specs=[
            pl.BlockSpec((1, per_block, n), lambda p: (p, 0, 0)),
            pl.BlockSpec((per_block, width, k_count), lambda p: (p, 0, 0)),
            pl.BlockSpec((per_block * width, n), lambda p: (p, 0)),
        ],
        out_specs=pl.BlockSpec((1, per_block * width, n), lambda p: (p, 0, 0)),
        out_shape=jax.ShapeDtypeStruct((blocks, per_block * width, n), jnp.bfloat16),
    )(codes_blocks, codebooks, base)


def gather_by_exchange(x, axis):
    count = lax.axis_size(axis)
    copies = jnp.broadcast_to(x[None], (count,) + x.shape)
    return lax.all_to_all(copies, axis, split_axis=0, concat_axis=0, tiled=True)


def local(queries, probe_groups, probe_cells, coarse, codebooks, codes, lengths, payload):
    groups = lax.axis_size("cell")
    parts = lax.axis_size("sub")
    capacity = CAP
    total = groups * capacity
    cell_dev = codes.shape[0]
    pw = payload.shape[2]
    chunk = pw // parts

    cell_count, sub_count, row_count = codes.shape
    rows_part = row_count // parts
    own_codes = codes.reshape(cell_count, sub_count, parts, rows_part)
    own_codes = jnp.transpose(own_codes, (2, 0, 1, 3)).astype(jnp.bfloat16).reshape(parts, -1, 128)
    tables = jnp.concatenate(
        [
            own_codes,
            jnp.broadcast_to(codebooks.reshape(1, -1, 128), (parts, codebooks.size // 128, 128)),
            jnp.broadcast_to(coarse.reshape(1, -1, 128), (parts, coarse.size // 128, 128)),
        ],
        axis=1,
    )
    tables = lax.all_to_all(tables, "sub", split_axis=0, concat_axis=0, tiled=True)
    tables = tables.reshape(parts, -1)
    code_size = own_codes.shape[1] * own_codes.shape[2]
    book_size = codebooks.size
    got_codes = tables[:, :code_size].reshape(parts, cell_count, sub_count, rows_part)
    got_codes = jnp.transpose(got_codes, (0, 2, 1, 3)).astype(jnp.int32)
    got_codes = got_codes.reshape(parts, sub_count, cell_count * rows_part)
    all_books = tables[:, code_size : code_size + book_size].reshape((-1,) + codebooks.shape[1:])
    all_coarse = tables[:, code_size + book_size :].reshape(parts, cell_count, -1)
    all_coarse = jnp.transpose(all_coarse, (1, 0, 2)).reshape(cell_count, -1)
    base = jnp.repeat(all_coarse.T, rows_part, axis=1)
    decoded_parts = decode(base, all_books, got_codes)

    slots = slot_table(probe_groups, groups, capacity)
    buffer, cell_marks = pack_slots(queries, probe_cells, slots, total)
    width = buffer.shape[1]
    arrived_all = lax.all_to_all(
        jnp.concatenate([buffer, cell_marks], axis=1).reshape(groups, -1),
        "cell",
        split_axis=0,
        concat_axis=0,
        tiled=True,
    ).reshape(total, -1)
    arrived = arrived_all[:, :width]
    arrived_cells = arrived_all[:, width:]
    query_parts = gather_by_exchange(arrived.T, "sub")
    decoded = decoded_parts.reshape(-1, decoded_parts.shape[2])
    cell_ids = arrived_cells.astype(jnp.int32)
    probed = jnp.any(
        cell_ids[:, :, None] == jnp.arange(cell_dev, dtype=jnp.int32)[None, None, :], axis=1
    )

    row_local = payload.shape[1]
    sq_norm = jnp.sum(jnp.square(decoded.astype(jnp.float32)), axis=0)
    first_row = lax.axis_index("sub") * row_local
    live = (first_row + jnp.arange(row_local, dtype=jnp.int32))[None, :] < lengths[:, None]
    keep = (probed[:, :, None] & live[None, :, :]).reshape(total, -1)
    table = payload.reshape(-1, pw)

    raw = jnp.einsum("sdq,sdr->qr", query_parts, decoded_parts, preferred_element_type=jnp.float32)
    values = (raw - 0.5 * sq_norm[None, :]) * score_scale
    local_peak = jnp.max(jnp.where(keep, values, floor_score), axis=1)
    weights = jnp.where(keep, jnp.exp(values - local_peak[:, None]), 0.0).astype(jnp.bfloat16)
    mass = jnp.sum(weights.astype(jnp.float32), axis=1)
    part_t = lax.dot_general(
        table, weights, (((0,), (1,)), ((), ())), preferred_element_type=jnp.float32
    )
    sendable = jnp.concatenate(
        [
            part_t.reshape(parts, chunk, total),
            jnp.broadcast_to(mass[None, None, :], (parts, 1, total)),
            jnp.broadcast_to(local_peak[None, None, :], (parts, 1, total)),
        ],
        axis=1,
    )
    pieces = lax.all_to_all(
        sendable.reshape(parts, -1, 128), "sub", split_axis=0, concat_axis=0, tiled=True
    ).reshape(parts, chunk + 2, -1, 128)
    peaks_in = pieces[:, chunk + 1]
    peak = jnp.max(peaks_in, axis=0)
    shift = jnp.exp(peaks_in - peak[None])
    reduced = jnp.sum(shift[:, None] * pieces[:, : chunk + 1], axis=0).reshape(chunk + 1, total)
    peak = peak.reshape(total)
    outgoing = jnp.concatenate([reduced, peak[None, :]], axis=0)
    back = lax.all_to_all(
        outgoing.reshape(chunk + 2, groups, capacity), "cell", split_axis=1, concat_axis=1, tiled=True
    )
    back = back.reshape(chunk + 2, total)
    picked = back[:, slots]
    parts_back = picked[:chunk]
    masses = picked[chunk]
    peaks = picked[chunk + 1]
    top = jnp.max(peaks, axis=1, keepdims=True)
    scale = jnp.exp(peaks - top)
    upper = jnp.sum(scale[None, :, :] * parts_back, axis=2)
    lower = jnp.sum(scale * masses, axis=1)
    pooled = (upper / lower[None, :]).T.astype(jnp.bfloat16)
    copies = jnp.broadcast_to(pooled[None], (parts,) + pooled.shape)
    gathered = lax.all_to_all(copies, "sub", split_axis=0, concat_axis=2, tiled=True)
    return gathered.reshape(pooled.shape[0], pw)


def solution(mesh):
    placed = (
        P("cell", "sub"),
        P("cell", None),
        P("cell", None, None),
        P("cell", "sub"),
        P("sub", None, None),
        P("cell", "sub", None),
        P("cell"),
        P("cell", "sub", None),
    )
    return jax.shard_map(
        local, mesh=mesh, in_specs=placed, out_specs=P("cell", None), check_vma=False
    )
```

```python
import jax
import jax.numpy as jnp
from jax import lax
from jax.experimental import pallas as pl
from jax.sharding import PartitionSpec as P


CAP = 64


score_scale = 0.3
floor_score = -1e30


def slot_table(probe_groups, groups, capacity):
    marks = (probe_groups[:, :, None] == jnp.arange(groups, dtype=jnp.int32)[None, None, :]).astype(
        jnp.int32
    )
    routed = jnp.sum(marks, axis=1)
    earlier = jnp.cumsum(routed, axis=0) - routed
    position = jnp.sum(marks * earlier[:, None, :], axis=2)
    return probe_groups * capacity + position


def pack_slots(rows, probe_cells, slots, total):
    flat = slots.reshape(-1)
    doubled = jnp.repeat(rows, 2, axis=0)
    buffer = jnp.zeros((total, rows.shape[1]), rows.dtype).at[flat].set(doubled)
    named = probe_cells.reshape(flat.shape[0], -1).astype(jnp.bfloat16)
    cell_marks = jnp.full((total, probe_cells.shape[2]), -1.0, jnp.bfloat16).at[flat].set(named)
    return (buffer, cell_marks)


def decode_kernel(codes_ref, book_ref, base_ref, out_ref):
    m_count, width, k_count = book_ref.shape
    n = codes_ref.shape[2]
    ids = lax.broadcasted_iota(jnp.int32, (k_count, n), 0)
    for m in range(m_count):
        row = codes_ref[0, m : m + 1, :]
        onehot = (ids == row).astype(jnp.bfloat16)
        val = jnp.dot(book_ref[m], onehot, preferred_element_type=jnp.float32)
        base = base_ref[m * width : (m + 1) * width, :].astype(jnp.float32)
        out_ref[0, m * width : (m + 1) * width, :] = (val + base).astype(jnp.bfloat16)


def decode(base, codebooks, codes_blocks):
    blocks, per_block, n = codes_blocks.shape
    width, k_count = codebooks.shape[1], codebooks.shape[2]
    return pl.pallas_call(
        decode_kernel,
        grid=(blocks,),
        in_specs=[
            pl.BlockSpec((1, per_block, n), lambda p: (p, 0, 0)),
            pl.BlockSpec((per_block, width, k_count), lambda p: (p, 0, 0)),
            pl.BlockSpec((per_block * width, n), lambda p: (p, 0)),
        ],
        out_specs=pl.BlockSpec((1, per_block * width, n), lambda p: (p, 0, 0)),
        out_shape=jax.ShapeDtypeStruct((blocks, per_block * width, n), jnp.bfloat16),
    )(codes_blocks, codebooks, base)


def gather_by_exchange(x, axis):
    count = lax.axis_size(axis)
    copies = jnp.broadcast_to(x[None], (count,) + x.shape)
    return lax.all_to_all(copies, axis, split_axis=0, concat_axis=0, tiled=True)


def local(queries, probe_groups, probe_cells, coarse, codebooks, codes, lengths, payload):
    groups = lax.axis_size("cell")
    parts = lax.axis_size("sub")
    capacity = CAP
    total = groups * capacity
    cell_dev = codes.shape[0]
    pw = payload.shape[2]
    chunk = pw // parts

    cell_count, sub_count, row_count = codes.shape
    rows_part = row_count // parts
    own_codes = codes.reshape(cell_count, sub_count, parts, rows_part)
    own_codes = jnp.transpose(own_codes, (2, 0, 1, 3)).astype(jnp.bfloat16).reshape(parts, -1, 128)
    tables = jnp.concatenate(
        [
            own_codes,
            jnp.broadcast_to(codebooks.reshape(1, -1, 128), (parts, codebooks.size // 128, 128)),
            jnp.broadcast_to(coarse.reshape(1, -1, 128), (parts, coarse.size // 128, 128)),
        ],
        axis=1,
    )
    tables = lax.all_to_all(tables, "sub", split_axis=0, concat_axis=0, tiled=True)
    tables = tables.reshape(parts, -1)
    code_size = own_codes.shape[1] * own_codes.shape[2]
    book_size = codebooks.size
    got_codes = tables[:, :code_size].reshape(parts, cell_count, sub_count, rows_part)
    got_codes = jnp.transpose(got_codes, (0, 2, 1, 3)).astype(jnp.int32)
    got_codes = got_codes.reshape(parts, sub_count, cell_count * rows_part)
    all_books = tables[:, code_size : code_size + book_size].reshape((-1,) + codebooks.shape[1:])
    all_coarse = tables[:, code_size + book_size :].reshape(parts, cell_count, -1)
    all_coarse = jnp.transpose(all_coarse, (1, 0, 2)).reshape(cell_count, -1)
    base = jnp.repeat(all_coarse.T, rows_part, axis=1)
    decoded_parts = decode(base, all_books, got_codes)

    slots = slot_table(probe_groups, groups, capacity)
    buffer, cell_marks = pack_slots(queries, probe_cells, slots, total)
    width = buffer.shape[1]
    outbound = jnp.concatenate([buffer, cell_marks], axis=1).T.reshape(-1, groups, capacity)
    arrived_all = lax.all_to_all(
        jnp.transpose(outbound, (1, 0, 2)).reshape(groups, -1),
        "cell",
        split_axis=0,
        concat_axis=0,
        tiled=True,
    ).reshape(groups, -1, capacity)
    arrived_all = jnp.transpose(arrived_all, (1, 0, 2)).reshape(-1, total)
    arrived_t = arrived_all[:width]
    arrived_cells = arrived_all[width:].T
    query_parts = gather_by_exchange(arrived_t, "sub")
    decoded = decoded_parts.reshape(-1, decoded_parts.shape[2])
    cell_ids = arrived_cells.astype(jnp.int32)
    probed = jnp.any(
        cell_ids[:, :, None] == jnp.arange(cell_dev, dtype=jnp.int32)[None, None, :], axis=1
    )

    row_local = payload.shape[1]
    sq_norm = jnp.sum(jnp.square(decoded.astype(jnp.float32)), axis=0)
    first_row = lax.axis_index("sub") * row_local
    live = (first_row + jnp.arange(row_local, dtype=jnp.int32))[None, :] < lengths[:, None]
    keep = (probed[:, :, None] & live[None, :, :]).reshape(total, -1)
    table = payload.reshape(-1, pw)

    raw = jnp.einsum("sdq,sdr->qr", query_parts, decoded_parts, preferred_element_type=jnp.float32)
    values = (raw - 0.5 * sq_norm[None, :]) * score_scale
    local_peak = jnp.max(jnp.where(keep, values, floor_score), axis=1)
    weights = jnp.where(keep, jnp.exp(values - local_peak[:, None]), 0.0).astype(jnp.bfloat16)
    mass = jnp.sum(weights.astype(jnp.float32), axis=1)
    part_t = lax.dot_general(
        table, weights, (((0,), (1,)), ((), ())), preferred_element_type=jnp.float32
    )
    sendable = jnp.concatenate(
        [
            part_t.reshape(parts, chunk, total),
            jnp.broadcast_to(mass[None, None, :], (parts, 1, total)),
            jnp.broadcast_to(local_peak[None, None, :], (parts, 1, total)),
        ],
        axis=1,
    )
    pieces = lax.all_to_all(
        sendable.reshape(parts, -1, 128), "sub", split_axis=0, concat_axis=0, tiled=True
    ).reshape(parts, chunk + 2, -1, 128)
    peaks_in = pieces[:, chunk + 1]
    peak = jnp.max(peaks_in, axis=0)
    shift = jnp.exp(peaks_in - peak[None])
    reduced = jnp.sum(shift[:, None] * pieces[:, : chunk + 1], axis=0).reshape(chunk + 1, total)
    peak = peak.reshape(total)
    outgoing = jnp.concatenate([reduced, peak[None, :]], axis=0)
    back = lax.all_to_all(
        outgoing.reshape(chunk + 2, groups, capacity), "cell", split_axis=1, concat_axis=1, tiled=True
    )
    back = back.reshape(chunk + 2, total)
    picked = back[:, slots]
    parts_back = picked[:chunk]
    masses = picked[chunk]
    peaks = picked[chunk + 1]
    top = jnp.max(peaks, axis=1, keepdims=True)
    scale = jnp.exp(peaks - top)
    upper = jnp.sum(scale[None, :, :] * parts_back, axis=2)
    lower = jnp.sum(scale * masses, axis=1)
    pooled = (upper / lower[None, :]).T.astype(jnp.bfloat16)
    copies = jnp.broadcast_to(pooled[None], (parts,) + pooled.shape)
    gathered = lax.all_to_all(copies, "sub", split_axis=0, concat_axis=2, tiled=True)
    return gathered.reshape(pooled.shape[0], pw)


def solution(mesh):
    placed = (
        P("cell", "sub"),
        P("cell", None),
        P("cell", None, None),
        P("cell", "sub"),
        P("sub", None, None),
        P("cell", "sub", None),
        P("cell"),
        P("cell", "sub", None),
    )
    return jax.shard_map(
        local, mesh=mesh, in_specs=placed, out_specs=P("cell", None), check_vma=False
    )
```

```python
import jax
import jax.numpy as jnp
from jax import lax
from jax.experimental import pallas as pl
from jax.sharding import PartitionSpec as P


CAP = 64


score_scale = 0.3
floor_score = -1e30


def slot_table(probe_groups, groups, capacity):
    marks = (probe_groups[:, :, None] == jnp.arange(groups, dtype=jnp.int32)[None, None, :]).astype(
        jnp.int32
    )
    routed = jnp.sum(marks, axis=1)
    earlier = jnp.cumsum(routed, axis=0) - routed
    position = jnp.sum(marks * earlier[:, None, :], axis=2)
    return probe_groups * capacity + position


def pack_slots(rows, probe_cells, slots, total):
    flat = slots.reshape(-1)
    doubled = jnp.repeat(rows, 2, axis=0)
    buffer = jnp.zeros((total, rows.shape[1]), rows.dtype).at[flat].set(doubled)
    named = probe_cells.reshape(flat.shape[0], -1).astype(jnp.bfloat16)
    cell_marks = jnp.full((total, probe_cells.shape[2]), -1.0, jnp.bfloat16).at[flat].set(named)
    return (buffer, cell_marks)


def decode_kernel(codes_ref, book_ref, base_ref, out_ref):
    m_count, width, k_count = book_ref.shape
    n = codes_ref.shape[2]
    ids = lax.broadcasted_iota(jnp.int32, (k_count, n), 0)
    for m in range(m_count):
        row = codes_ref[0, m : m + 1, :]
        onehot = (ids == row).astype(jnp.bfloat16)
        val = jnp.dot(book_ref[m], onehot, preferred_element_type=jnp.float32)
        base = base_ref[m * width : (m + 1) * width, :].astype(jnp.float32)
        out_ref[0, m * width : (m + 1) * width, :] = (val + base).astype(jnp.bfloat16)


def decode(base, codebooks, codes_blocks):
    blocks, per_block, n = codes_blocks.shape
    width, k_count = codebooks.shape[1], codebooks.shape[2]
    return pl.pallas_call(
        decode_kernel,
        grid=(blocks,),
        in_specs=[
            pl.BlockSpec((1, per_block, n), lambda p: (p, 0, 0)),
            pl.BlockSpec((per_block, width, k_count), lambda p: (p, 0, 0)),
            pl.BlockSpec((per_block * width, n), lambda p: (p, 0)),
        ],
        out_specs=pl.BlockSpec((1, per_block * width, n), lambda p: (p, 0, 0)),
        out_shape=jax.ShapeDtypeStruct((blocks, per_block * width, n), jnp.bfloat16),
    )(codes_blocks, codebooks, base)


def gather_by_exchange(x, axis):
    count = lax.axis_size(axis)
    copies = jnp.broadcast_to(x[None], (count,) + x.shape)
    return lax.all_to_all(copies, axis, split_axis=0, concat_axis=0, tiled=True)


def local(queries, probe_groups, probe_cells, coarse, codebooks, codes, lengths, payload):
    groups = lax.axis_size("cell")
    parts = lax.axis_size("sub")
    capacity = CAP
    total = groups * capacity
    cell_dev = codes.shape[0]
    pw = payload.shape[2]
    chunk = pw // parts

    cell_count, sub_count, row_count = codes.shape
    rows_part = row_count // parts
    own_codes = codes.reshape(cell_count, sub_count, parts, rows_part)
    own_codes = jnp.transpose(own_codes, (2, 0, 1, 3)).astype(jnp.bfloat16).reshape(parts, -1, 128)
    tables = jnp.concatenate(
        [
            own_codes,
            jnp.broadcast_to(codebooks.reshape(1, -1, 128), (parts, codebooks.size // 128, 128)),
            jnp.broadcast_to(coarse.reshape(1, -1, 128), (parts, coarse.size // 128, 128)),
        ],
        axis=1,
    )
    tables = lax.all_to_all(tables, "sub", split_axis=0, concat_axis=0, tiled=True)
    tables = tables.reshape(parts, -1)
    code_size = own_codes.shape[1] * own_codes.shape[2]
    book_size = codebooks.size
    got_codes = tables[:, :code_size].reshape(parts, cell_count, sub_count, rows_part)
    got_codes = jnp.transpose(got_codes, (0, 2, 1, 3)).astype(jnp.int32)
    got_codes = got_codes.reshape(parts, sub_count, cell_count * rows_part)
    all_books = tables[:, code_size : code_size + book_size].reshape((-1,) + codebooks.shape[1:])
    all_coarse = tables[:, code_size + book_size :].reshape(parts, cell_count, -1)
    all_coarse = jnp.transpose(all_coarse, (1, 0, 2)).reshape(cell_count, -1)
    base = jnp.repeat(all_coarse.T, rows_part, axis=1)
    decoded_parts = decode(base, all_books, got_codes)

    slots = slot_table(probe_groups, groups, capacity)
    buffer, cell_marks = pack_slots(queries, probe_cells, slots, total)
    width = buffer.shape[1]
    outbound = jnp.concatenate([buffer, cell_marks], axis=1).T.reshape(-1, groups, capacity)
    arrived_all = lax.all_to_all(
        jnp.transpose(outbound, (1, 0, 2)).reshape(groups, -1),
        "cell",
        split_axis=0,
        concat_axis=0,
        tiled=True,
    ).reshape(groups, -1, capacity)
    arrived_all = jnp.transpose(arrived_all, (1, 0, 2)).reshape(-1, total)
    arrived_t = arrived_all[:width]
    arrived_cells = arrived_all[width:].T
    query_parts = gather_by_exchange(arrived_t, "sub")
    decoded = decoded_parts.reshape(-1, decoded_parts.shape[2])
    cell_ids = arrived_cells.astype(jnp.int32)
    probed = jnp.any(
        cell_ids[:, :, None] == jnp.arange(cell_dev, dtype=jnp.int32)[None, None, :], axis=1
    )

    row_local = payload.shape[1]
    sq_norm = jnp.sum(jnp.square(decoded.astype(jnp.float32)), axis=0)
    first_row = lax.axis_index("sub") * row_local
    live = (first_row + jnp.arange(row_local, dtype=jnp.int32))[None, :] < lengths[:, None]
    keep = (probed[:, :, None] & live[None, :, :]).reshape(total, -1)
    table = payload.reshape(-1, pw)

    raw = jnp.einsum("sdq,sdr->qr", query_parts, decoded_parts, preferred_element_type=jnp.float32)
    values = (raw - 0.5 * sq_norm[None, :]) * score_scale
    local_peak = jnp.max(jnp.where(keep, values, floor_score), axis=1)
    weights = jnp.where(keep, jnp.exp(values - local_peak[:, None]), 0.0).astype(jnp.bfloat16)
    mass = jnp.sum(weights.astype(jnp.float32), axis=1)
    part_t = lax.dot_general(
        table, weights, (((0,), (1,)), ((), ())), preferred_element_type=jnp.float32
    )
    sendable = jnp.concatenate(
        [
            part_t.reshape(parts, chunk, total),
            jnp.broadcast_to(mass[None, None, :], (parts, 1, total)),
            jnp.broadcast_to(local_peak[None, None, :], (parts, 1, total)),
        ],
        axis=1,
    )
    pieces = lax.all_to_all(
        sendable.reshape(parts, -1, 128), "sub", split_axis=0, concat_axis=0, tiled=True
    ).reshape(parts, chunk + 2, -1, 128)
    peaks_in = pieces[:, chunk + 1]
    peak = jnp.max(peaks_in, axis=0)
    shift = jnp.exp(peaks_in - peak[None])
    reduced = jnp.sum(shift[:, None] * pieces[:, : chunk + 1], axis=0)
    outgoing = jnp.concatenate([reduced, peak[None]], axis=0)
    outgoing = outgoing.reshape(chunk + 2, total).reshape(chunk + 2, groups, capacity)
    outgoing = jnp.transpose(outgoing, (1, 0, 2)).reshape(groups, -1)
    back = lax.all_to_all(outgoing, "cell", split_axis=0, concat_axis=0, tiled=True)
    back = jnp.transpose(back.reshape(groups, chunk + 2, capacity), (1, 0, 2)).reshape(chunk + 2, total)
    picked = back[:, slots]
    parts_back = picked[:chunk]
    masses = picked[chunk]
    peaks = picked[chunk + 1]
    top = jnp.max(peaks, axis=1, keepdims=True)
    scale = jnp.exp(peaks - top)
    upper = jnp.sum(scale[None, :, :] * parts_back, axis=2)
    lower = jnp.sum(scale * masses, axis=1)
    pooled = (upper / lower[None, :]).T.astype(jnp.bfloat16)
    copies = jnp.broadcast_to(pooled[None], (parts,) + pooled.shape)
    gathered = lax.all_to_all(copies, "sub", split_axis=0, concat_axis=2, tiled=True)
    return gathered.reshape(pooled.shape[0], pw)


def solution(mesh):
    placed = (
        P("cell", "sub"),
        P("cell", None),
        P("cell", None, None),
        P("cell", "sub"),
        P("sub", None, None),
        P("cell", "sub", None),
        P("cell"),
        P("cell", "sub", None),
    )
    return jax.shard_map(
        local, mesh=mesh, in_specs=placed, out_specs=P("cell", None), check_vma=False
    )
```

```python
import jax
import jax.numpy as jnp
from jax import lax
from jax.experimental import pallas as pl
from jax.sharding import PartitionSpec as P


CAP = 64


score_scale = 0.3
floor_score = -1e30


def slot_table(probe_groups, groups, capacity):
    marks = (probe_groups[:, :, None] == jnp.arange(groups, dtype=jnp.int32)[None, None, :]).astype(
        jnp.int32
    )
    routed = jnp.sum(marks, axis=1)
    earlier = jnp.cumsum(routed, axis=0) - routed
    position = jnp.sum(marks * earlier[:, None, :], axis=2)
    return probe_groups * capacity + position


def pack_slots(rows, probe_cells, slots, total):
    flat = slots.reshape(-1)
    doubled = jnp.repeat(rows, 2, axis=0)
    buffer = jnp.zeros((total, rows.shape[1]), rows.dtype).at[flat].set(doubled)
    named = probe_cells.reshape(flat.shape[0], -1).astype(jnp.bfloat16)
    cell_marks = jnp.full((total, probe_cells.shape[2]), -1.0, jnp.bfloat16).at[flat].set(named)
    return (buffer, cell_marks)


def decode_kernel(codes_ref, book_ref, base_ref, out_ref):
    m_count, width, k_count = book_ref.shape
    n = codes_ref.shape[2]
    ids = lax.broadcasted_iota(jnp.int32, (k_count, n), 0)
    for m in range(m_count):
        row = codes_ref[0, m : m + 1, :]
        onehot = (ids == row).astype(jnp.bfloat16)
        val = jnp.dot(book_ref[m], onehot, preferred_element_type=jnp.float32)
        base = base_ref[m * width : (m + 1) * width, :].astype(jnp.float32)
        out_ref[0, m * width : (m + 1) * width, :] = (val + base).astype(jnp.bfloat16)


def decode(base, codebooks, codes_blocks):
    blocks, per_block, n = codes_blocks.shape
    width, k_count = codebooks.shape[1], codebooks.shape[2]
    return pl.pallas_call(
        decode_kernel,
        grid=(blocks,),
        in_specs=[
            pl.BlockSpec((1, per_block, n), lambda p: (p, 0, 0)),
            pl.BlockSpec((per_block, width, k_count), lambda p: (p, 0, 0)),
            pl.BlockSpec((per_block * width, n), lambda p: (p, 0)),
        ],
        out_specs=pl.BlockSpec((1, per_block * width, n), lambda p: (p, 0, 0)),
        out_shape=jax.ShapeDtypeStruct((blocks, per_block * width, n), jnp.bfloat16),
    )(codes_blocks, codebooks, base)


def gather_by_exchange(x, axis):
    count = lax.axis_size(axis)
    copies = jnp.broadcast_to(x[None], (count,) + x.shape)
    return lax.all_to_all(copies, axis, split_axis=0, concat_axis=0, tiled=True)


def local(queries, probe_groups, probe_cells, coarse, codebooks, codes, lengths, payload):
    groups = lax.axis_size("cell")
    parts = lax.axis_size("sub")
    capacity = CAP
    total = groups * capacity
    cell_dev = codes.shape[0]
    pw = payload.shape[2]
    chunk = pw // parts

    cell_count, sub_count, row_count = codes.shape
    rows_part = row_count // parts
    own_codes = codes.reshape(cell_count, sub_count, parts, rows_part)
    own_codes = lax.optimization_barrier(jnp.transpose(own_codes, (2, 0, 1, 3)).reshape(parts, -1, 128))
    own_codes = own_codes.astype(jnp.bfloat16)
    tables = jnp.concatenate(
        [
            own_codes,
            jnp.broadcast_to(codebooks.reshape(1, -1, 128), (parts, codebooks.size // 128, 128)),
            jnp.broadcast_to(coarse.reshape(1, -1, 128), (parts, coarse.size // 128, 128)),
        ],
        axis=1,
    )
    tables = lax.all_to_all(tables, "sub", split_axis=0, concat_axis=0, tiled=True)
    tables = tables.reshape(parts, -1)
    code_size = own_codes.shape[1] * own_codes.shape[2]
    book_size = codebooks.size
    got_codes = tables[:, :code_size].reshape(parts, cell_count, sub_count, rows_part)
    got_codes = jnp.transpose(got_codes, (0, 2, 1, 3)).astype(jnp.int32)
    got_codes = got_codes.reshape(parts, sub_count, cell_count * rows_part)
    all_books = tables[:, code_size : code_size + book_size].reshape((-1,) + codebooks.shape[1:])
    all_coarse = tables[:, code_size + book_size :].reshape(parts, cell_count, -1)
    all_coarse = jnp.transpose(all_coarse, (1, 0, 2)).reshape(cell_count, -1)
    base = jnp.repeat(all_coarse.T, rows_part, axis=1)
    decoded_parts = decode(base, all_books, got_codes)

    slots = slot_table(probe_groups, groups, capacity)
    buffer, cell_marks = pack_slots(queries, probe_cells, slots, total)
    width = buffer.shape[1]
    outbound = jnp.concatenate([buffer, cell_marks], axis=1).T.reshape(-1, groups, capacity)
    arrived_all = lax.all_to_all(
        jnp.transpose(outbound, (1, 0, 2)).reshape(groups, 2, -1),
        "cell",
        split_axis=0,
        concat_axis=0,
        tiled=True,
    ).reshape(groups, -1, capacity)
    arrived_all = jnp.transpose(arrived_all, (1, 0, 2)).reshape(-1, total)
    arrived_t = arrived_all[:width]
    arrived_cells = arrived_all[width:].T
    query_parts = gather_by_exchange(arrived_t, "sub")
    decoded = decoded_parts.reshape(-1, decoded_parts.shape[2])
    cell_ids = arrived_cells.astype(jnp.int32)
    probed = jnp.any(
        cell_ids[:, :, None] == jnp.arange(cell_dev, dtype=jnp.int32)[None, None, :], axis=1
    )

    row_local = payload.shape[1]
    sq_norm = jnp.sum(jnp.square(decoded.astype(jnp.float32)), axis=0)
    first_row = lax.axis_index("sub") * row_local
    live = (first_row + jnp.arange(row_local, dtype=jnp.int32))[None, :] < lengths[:, None]
    keep = (probed[:, :, None] & live[None, :, :]).reshape(total, -1)
    table = payload.reshape(-1, pw)

    raw = jnp.einsum("sdq,sdr->qr", query_parts, decoded_parts, preferred_element_type=jnp.float32)
    values = (raw - 0.5 * sq_norm[None, :]) * score_scale
    local_peak = jnp.max(jnp.where(keep, values, floor_score), axis=1)
    weights = jnp.where(keep, jnp.exp(values - local_peak[:, None]), 0.0).astype(jnp.bfloat16)
    mass = jnp.sum(weights.astype(jnp.float32), axis=1)
    part_t = lax.dot_general(
        table, weights, (((0,), (1,)), ((), ())), preferred_element_type=jnp.float32
    )
    sendable = jnp.concatenate(
        [
            part_t.reshape(parts, chunk, total),
            jnp.broadcast_to(mass[None, None, :], (parts, 1, total)),
            jnp.broadcast_to(local_peak[None, None, :], (parts, 1, total)),
        ],
        axis=1,
    )
    pieces = lax.all_to_all(
        sendable.reshape(parts, -1, 128), "sub", split_axis=0, concat_axis=0, tiled=True
    ).reshape(parts, chunk + 2, -1, 128)
    peaks_in = pieces[:, chunk + 1]
    peak = jnp.max(peaks_in, axis=0)
    shift = jnp.exp(peaks_in - peak[None])
    reduced = jnp.sum(shift[:, None] * pieces[:, : chunk + 1], axis=0)
    outgoing = jnp.concatenate([reduced, peak[None]], axis=0)
    outgoing = outgoing.reshape(chunk + 2, total).reshape(chunk + 2, groups, capacity)
    outgoing = jnp.transpose(outgoing, (1, 0, 2)).reshape(groups, -1)
    back = lax.all_to_all(outgoing, "cell", split_axis=0, concat_axis=0, tiled=True)
    back = jnp.transpose(back.reshape(groups, chunk + 2, capacity), (1, 0, 2)).reshape(chunk + 2, total)
    picked = back[:, slots]
    parts_back = picked[:chunk]
    masses = picked[chunk]
    peaks = picked[chunk + 1]
    top = jnp.max(peaks, axis=1, keepdims=True)
    scale = jnp.exp(peaks - top)
    upper = jnp.sum(scale[None, :, :] * parts_back, axis=2)
    lower = jnp.sum(scale * masses, axis=1)
    pooled = (upper / lower[None, :]).T.astype(jnp.bfloat16)
    copies = jnp.broadcast_to(pooled[None], (parts,) + pooled.shape)
    gathered = lax.all_to_all(copies, "sub", split_axis=0, concat_axis=2, tiled=True)
    return gathered.reshape(pooled.shape[0], pw)


def solution(mesh):
    placed = (
        P("cell", "sub"),
        P("cell", None),
        P("cell", None, None),
        P("cell", "sub"),
        P("sub", None, None),
        P("cell", "sub", None),
        P("cell"),
        P("cell", "sub", None),
    )
    return jax.shard_map(
        local, mesh=mesh, in_specs=placed, out_specs=P("cell", None), check_vma=False
    )
```

```python
import jax
import jax.numpy as jnp
from jax import lax
from jax.experimental import pallas as pl
from jax.sharding import PartitionSpec as P


CAP = 64


score_scale = 0.3
floor_score = -1e30


def slot_table(probe_groups, groups, capacity):
    marks = (probe_groups[:, :, None] == jnp.arange(groups, dtype=jnp.int32)[None, None, :]).astype(
        jnp.int32
    )
    routed = jnp.sum(marks, axis=1)
    earlier = jnp.cumsum(routed, axis=0) - routed
    position = jnp.sum(marks * earlier[:, None, :], axis=2)
    return probe_groups * capacity + position


def pack_slots(rows, probe_cells, slots, total):
    flat = slots.reshape(-1)
    doubled = jnp.repeat(rows, 2, axis=0)
    buffer = jnp.zeros((total, rows.shape[1]), rows.dtype).at[flat].set(doubled)
    named = probe_cells.reshape(flat.shape[0], -1).astype(jnp.bfloat16)
    cell_marks = jnp.full((total, probe_cells.shape[2]), -1.0, jnp.bfloat16).at[flat].set(named)
    return (buffer, cell_marks)


def decode_kernel(codes_ref, book_ref, base_ref, out_ref):
    m_count, width, k_count = book_ref.shape
    n = codes_ref.shape[2]
    ids = lax.broadcasted_iota(jnp.int32, (k_count, n), 0)
    for m in range(m_count):
        row = codes_ref[0, m : m + 1, :]
        onehot = (ids == row).astype(jnp.bfloat16)
        val = jnp.dot(book_ref[m], onehot, preferred_element_type=jnp.float32)
        base = base_ref[m * width : (m + 1) * width, :].astype(jnp.float32)
        out_ref[0, m * width : (m + 1) * width, :] = (val + base).astype(jnp.bfloat16)


def decode(base, codebooks, codes_blocks):
    blocks, per_block, n = codes_blocks.shape
    width, k_count = codebooks.shape[1], codebooks.shape[2]
    return pl.pallas_call(
        decode_kernel,
        grid=(blocks,),
        in_specs=[
            pl.BlockSpec((1, per_block, n), lambda p: (p, 0, 0)),
            pl.BlockSpec((per_block, width, k_count), lambda p: (p, 0, 0)),
            pl.BlockSpec((per_block * width, n), lambda p: (p, 0)),
        ],
        out_specs=pl.BlockSpec((1, per_block * width, n), lambda p: (p, 0, 0)),
        out_shape=jax.ShapeDtypeStruct((blocks, per_block * width, n), jnp.bfloat16),
    )(codes_blocks, codebooks, base)


def gather_by_exchange(x, axis):
    count = lax.axis_size(axis)
    copies = jnp.broadcast_to(x[None], (count,) + x.shape)
    return lax.all_to_all(copies, axis, split_axis=0, concat_axis=0, tiled=True)


def local(queries, probe_groups, probe_cells, coarse, codebooks, codes, lengths, payload):
    groups = lax.axis_size("cell")
    parts = lax.axis_size("sub")
    capacity = CAP
    total = groups * capacity
    cell_dev = codes.shape[0]
    pw = payload.shape[2]
    chunk = pw // parts

    cell_count, sub_count, row_count = codes.shape
    rows_part = row_count // parts
    own_codes = codes.reshape(cell_count, sub_count, parts, rows_part)
    own_codes = jnp.transpose(own_codes, (2, 0, 1, 3)).astype(jnp.bfloat16).reshape(parts, -1, 128)
    tables = jnp.concatenate(
        [
            own_codes,
            jnp.broadcast_to(codebooks.reshape(1, -1, 128), (parts, codebooks.size // 128, 128)),
            jnp.broadcast_to(coarse.reshape(1, -1, 128), (parts, coarse.size // 128, 128)),
        ],
        axis=1,
    )
    tables = lax.all_to_all(tables, "sub", split_axis=0, concat_axis=0, tiled=True)
    tables = tables.reshape(parts, -1)
    code_size = own_codes.shape[1] * own_codes.shape[2]
    book_size = codebooks.size
    got_codes = tables[:, :code_size].reshape(parts, cell_count, sub_count, rows_part)
    got_codes = jnp.transpose(got_codes, (0, 2, 1, 3)).astype(jnp.int32)
    got_codes = got_codes.reshape(parts, sub_count, cell_count * rows_part)
    all_books = tables[:, code_size : code_size + book_size].reshape((-1,) + codebooks.shape[1:])
    all_coarse = tables[:, code_size + book_size :].reshape(parts, cell_count, -1)
    all_coarse = jnp.transpose(all_coarse, (1, 0, 2)).reshape(cell_count, -1)
    base = jnp.repeat(all_coarse.T, rows_part, axis=1)
    decoded_parts = decode(base, all_books, got_codes)

    slots = slot_table(probe_groups, groups, capacity)
    buffer, cell_marks = pack_slots(queries, probe_cells, slots, total)
    width = buffer.shape[1]
    outbound = jnp.concatenate([buffer, cell_marks], axis=1).T.reshape(-1, groups, capacity)
    arrived_all = lax.all_to_all(
        jnp.transpose(outbound, (1, 0, 2)).reshape(groups, 2, -1),
        "cell",
        split_axis=0,
        concat_axis=0,
        tiled=True,
    ).reshape(groups, -1, capacity)
    arrived_all = jnp.transpose(arrived_all, (1, 0, 2)).reshape(-1, total)
    arrived_t = arrived_all[:width]
    arrived_cells = arrived_all[width:].T
    query_parts = gather_by_exchange(arrived_t, "sub")
    decoded = decoded_parts.reshape(-1, decoded_parts.shape[2])
    cell_ids = arrived_cells.astype(jnp.int32)
    probed = jnp.any(
        cell_ids[:, :, None] == jnp.arange(cell_dev, dtype=jnp.int32)[None, None, :], axis=1
    )

    row_local = payload.shape[1]
    sq_norm = jnp.sum(jnp.square(decoded.astype(jnp.float32)), axis=0)
    first_row = lax.axis_index("sub") * row_local
    live = (first_row + jnp.arange(row_local, dtype=jnp.int32))[None, :] < lengths[:, None]
    keep = (probed[:, :, None] & live[None, :, :]).reshape(total, -1)
    table = payload.reshape(-1, pw)

    raw = jnp.einsum("sdq,sdr->qr", query_parts, decoded_parts, preferred_element_type=jnp.float32)
    values = (raw - 0.5 * sq_norm[None, :]) * score_scale
    local_peak = jnp.max(jnp.where(keep, values, floor_score), axis=1)
    weights = jnp.where(keep, jnp.exp(values - local_peak[:, None]), 0.0).astype(jnp.bfloat16)
    mass = jnp.sum(weights.astype(jnp.float32), axis=1)
    part_t = lax.dot_general(
        table, weights, (((0,), (1,)), ((), ())), preferred_element_type=jnp.float32
    )
    sendable = jnp.concatenate(
        [
            part_t.reshape(parts, chunk, total),
            jnp.broadcast_to(mass[None, None, :], (parts, 1, total)),
            jnp.broadcast_to(local_peak[None, None, :], (parts, 1, total)),
        ],
        axis=1,
    )
    pieces = lax.all_to_all(
        sendable.reshape(parts, -1, 128), "sub", split_axis=0, concat_axis=0, tiled=True
    ).reshape(parts, chunk + 2, -1, 128)
    peaks_in = pieces[:, chunk + 1]
    peak = jnp.max(peaks_in, axis=0)
    shift = jnp.exp(peaks_in - peak[None])
    reduced = jnp.sum(shift[:, None] * pieces[:, : chunk + 1], axis=0)
    outgoing = jnp.concatenate([reduced, peak[None]], axis=0)
    outgoing = outgoing.reshape(chunk + 2, total).reshape(chunk + 2, groups, capacity)
    outgoing = jnp.transpose(outgoing, (1, 0, 2)).reshape(groups, -1)
    back = lax.all_to_all(outgoing, "cell", split_axis=0, concat_axis=0, tiled=True)
    back = jnp.transpose(back.reshape(groups, chunk + 2, capacity), (1, 0, 2)).reshape(chunk + 2, total)
    picked = back[:, slots]
    parts_back = picked[:chunk]
    masses = picked[chunk]
    peaks = picked[chunk + 1]
    top = jnp.max(peaks, axis=1, keepdims=True)
    scale = jnp.exp(peaks - top)
    upper = jnp.sum(scale[None, :, :] * parts_back, axis=2)
    lower = jnp.sum(scale * masses, axis=1)
    pooled = (upper / lower[None, :]).T.astype(jnp.bfloat16)
    copies = jnp.broadcast_to(pooled.reshape(1, 2, -1), (parts, 2, pooled.size // 2))
    gathered = lax.all_to_all(copies, "sub", split_axis=0, concat_axis=0, tiled=True)
    gathered = gathered.reshape((parts,) + pooled.shape)
    return jnp.transpose(gathered, (1, 0, 2)).reshape(pooled.shape[0], pw)


def solution(mesh):
    placed = (
        P("cell", "sub"),
        P("cell", None),
        P("cell", None, None),
        P("cell", "sub"),
        P("sub", None, None),
        P("cell", "sub", None),
        P("cell"),
        P("cell", "sub", None),
    )
    return jax.shard_map(
        local, mesh=mesh, in_specs=placed, out_specs=P("cell", None), check_vma=False
    )
```
